32 devices in a mesh: pair: 16 (over z, y, x), vtile: 1, irrep: 2 (over core).
Axes of the slice: x: 2, y: 2, z: 4, core: 2. Of those that a mesh axis runs over, the one named last changes fastest.
Arguments:
- amplitudes: bfloat16 [80, 8, 7744], P('pair'), may hold values from -4 to 4
- slabs: bfloat16 [16, 8, 2, 88, 7744], P('pair', 'vtile', 'irrep'), may hold values from -1.5 to 1.5
- couplings: bfloat16 [2, 30, 30, 176], P(None, None, None, 'irrep'), may hold values from -6 to 6
- occ_energy: float32 [30], replicated, may hold values from -2 to -0.3
- vir_energy: float32 [8, 88], replicated, may hold values from 0.2 to 4
- occ_irrep: int32 [30], replicated, may hold values from 0 to 7
- pair_i: int32 [80], P('pair'), may hold values from 0 to 29, as said below
- pair_j: int32 [80], P('pair'), may hold values from 0 to 29, as said below
- window_k: int32 [2], replicated, may hold values from 0 to 29
- owner: int32 [2], replicated, may hold values from 0 to 15
Outputs:
- resid_part: float32 [80, 8, 7744], P('pair', 'vtile', 'irrep')
The draws below stay inside these ranges and needn't reach their ends.
Inputs may be any that keep to these rules, and one draw needn't show every extreme that they name: Pairs come in groups of 16 that share pair_i; groups have different pair_i. Within a group of pairs sharing pair_i, pair_j values are distinct.
All inputs are finite; a program needn't handle non-finite values.
Results may differ from the reference program's by a relative error of at most 0.0003.
Values may be sent and summed in bfloat16 or wider, within the bound.
No kernel may reach another device: no remote copies, remote signals or barrier semaphores. Data moves between devices by JAX's collectives and lax.ppermute only.
A program may use at most 256 MiB of HBM per device.

```python
import jax
import jax.numpy as jnp
from jax import lax

VBLK = 88
NOCC = 30
K_WIN = 2
PAIRS = 80
SLOTS = 16
CWIN = 2


def pair_table(key):
    base_key = jax.random.fold_in(key, 7)
    first_key, second_key, slot_key = jax.random.split(base_key, 3)
    groups = PAIRS // 16
    middle_first = (jax.random.permutation(first_key, NOCC - 2)[:groups - 2] + 1).astype(jnp.int32)
    firsts = jnp.concatenate([jnp.array([0, NOCC - 1], jnp.int32), middle_first])
    group_keys = jax.random.split(second_key, groups)

    def group_seconds(member):
        middle = (jax.random.permutation(member, NOCC - 2)[:14] + 1).astype(jnp.int32)
        return jnp.concatenate([jnp.array([0, NOCC - 1], jnp.int32), middle])
    seconds = jax.vmap(group_seconds)(group_keys)
    slots = jax.random.permutation(slot_key, PAIRS)
    flat_first = jnp.repeat(firsts, 16).astype(jnp.int32)
    flat_second = seconds.reshape(-1).astype(jnp.int32)
    first_out = jnp.zeros((PAIRS,), jnp.int32).at[slots].set(flat_first)
    second_out = jnp.zeros((PAIRS,), jnp.int32).at[slots].set(flat_second)
    return (first_out, second_out)


def draw_pair_i(key, part):
    return pair_table(key)[0]


def draw_pair_j(key, part):
    return pair_table(key)[1]


def with_ends(result, key, smallest, top_value):
    dims = result.shape
    place = [jax.random.randint(jax.random.fold_in(key, axis), (), 0, dims[axis]) for axis in range(len(dims))]
    result = result.at[tuple(place)].set(smallest)
    longest = dims.index(max(dims))
    place[longest] = (place[longest] + 1) % dims[longest]
    return result.at[tuple(place)].set(top_value)


def block_scale(rng, extent, pieces, smallest, high):
    level, own = 1.0, jax.random.fold_in(rng, 6)
    for dim, parts in pieces:
        steps = jnp.exp(jax.random.uniform(jax.random.fold_in(own, dim), (parts,), jnp.float32, smallest / len(pieces), high / len(pieces)))
        level = level * jnp.repeat(steps, extent[dim] // parts).reshape([-1 if axis == dim else 1 for axis in range(len(extent))])
    return level


def normal_values(rng, shape, scale, limit, pieces=(), kind=jnp.bfloat16):
    level = block_scale(rng, shape, pieces, -0.22, 0.18) if pieces else 1.0
    entries = jax.random.normal(rng, shape, jnp.float32) * scale * level
    return jnp.minimum(jnp.maximum(entries, -limit), limit).astype(kind)


def setup_inputs(seed: int = 0) -> dict:
    key_list = jax.random.split(jax.random.key(seed), 11)
    return {
        "amplitudes": normal_values(key_list[0], (PAIRS, 8, VBLK * VBLK), 0.3, 4.0, ((0, 16),)),
        "slabs": normal_values(key_list[1], (SLOTS, 8, CWIN, VBLK, VBLK * VBLK), 0.1, 1.5, ((0, 16), (2, 2))),
        "couplings": normal_values(key_list[2], (K_WIN, NOCC, NOCC, CWIN * VBLK), 0.7, 6.0, ((3, 2),)),
        "occ_energy": jnp.clip(jax.random.uniform(key_list[3], (NOCC,), jnp.float32, -2.0, -0.3), -2.0, -0.3),
        "vir_energy": jnp.clip(jax.random.uniform(key_list[4], (8, VBLK), jnp.float32, 0.2, 4.0), 0.2, 4.0),
        "occ_irrep": with_ends(jax.random.randint(key_list[5], (NOCC,), 0, 8), jax.random.fold_in(key_list[5], 1), 0, 7).astype(jnp.int32),
        "pair_i": draw_pair_i(jax.random.fold_in(key_list[10], 71), 0),
        "pair_j": draw_pair_j(jax.random.fold_in(key_list[10], 71), 0),
        "window_k": jax.random.randint(key_list[8], (K_WIN,), 0, NOCC).astype(jnp.int32),
        "owner": jax.random.randint(key_list[9], (K_WIN,), 0, SLOTS).astype(jnp.int32),
    }


def reference(amplitudes, slabs, couplings, occ_energy, vir_energy, occ_irrep, pair_i, pair_j, window_k, owner):
    highest = lax.Precision.HIGHEST
    blocks = jnp.arange(8, dtype=jnp.int32)
    gammas = jnp.arange(CWIN, dtype=jnp.int32)
    pair_sym = jnp.bitwise_xor(occ_irrep[pair_i], occ_irrep[pair_j])
    selector = jnp.bitwise_xor(blocks[:, None], pair_sym[None, :])
    hole_amp = amplitudes[jnp.arange(PAIRS, dtype=jnp.int32)[None, :], selector].astype(jnp.float32)

    def one_pair(packed):
        amp_pair, occ_i, occ_j = packed
        pair_irrep = jnp.bitwise_xor(occ_irrep[occ_i], occ_irrep[occ_j])
        accumulated = jnp.zeros((8, VBLK * VBLK), jnp.float32)
        for window in range(K_WIN):
            k_index = window_k[window]
            k_irrep = occ_irrep[k_index]
            slab_data = jnp.take(slabs, owner[window], axis=0).astype(jnp.float32)
            alpha_irrep = jnp.bitwise_xor(jnp.bitwise_xor(pair_irrep, k_irrep), jnp.bitwise_xor(blocks[:, None], gammas[None, :]))
            amp_sel = amp_pair[alpha_irrep].reshape(8, CWIN, VBLK, VBLK).astype(jnp.float32)
            particle = jnp.einsum('bgad,bgdx->bgax', amp_sel, slab_data, precision=highest)
            y_column = jnp.take(couplings[window], occ_j, axis=1).reshape(NOCC, CWIN, VBLK)
            keep_mask = jnp.bitwise_xor(jnp.bitwise_xor(occ_irrep[:, None], gammas[None, :]), jnp.bitwise_xor(occ_irrep[occ_j], k_irrep)) == 0
            coef_rows = y_column.astype(jnp.float32) * keep_mask[:, :, None].astype(jnp.float32)
            coupling = (coef_rows[pair_j] * (pair_i == occ_i).astype(jnp.float32)[:, None, None]).astype(jnp.bfloat16)
            hole_part = jnp.einsum('bqx,qgc->bgxc', hole_amp, coupling.astype(jnp.float32), precision=highest)
            hole_part = hole_part.reshape(8, CWIN, VBLK, VBLK * VBLK)
            energy_a = vir_energy[alpha_irrep]
            energy_b = vir_energy
            energy_c = vir_energy[gammas]
            base = occ_energy[occ_i] + occ_energy[occ_j] + occ_energy[k_index]
            denominator = energy_a[:, :, :, None, None] + energy_b[:, None, None, :, None] + energy_c[None, :, None, None, :] - base
            triples = ((particle - hole_part) / denominator.reshape(8, CWIN, VBLK, VBLK * VBLK)).astype(jnp.bfloat16)
            contrib = jnp.einsum('bgax,bgdx->bgad', triples.astype(jnp.float32), slab_data, precision=highest)
            accumulated = accumulated.at[alpha_irrep.reshape(-1)].add(contrib.reshape(8 * CWIN, VBLK * VBLK))
        return accumulated

    return lax.map(one_pair, (amplitudes, pair_i, pair_j))
```

```python
import math

import jax
import jax.numpy as jnp
from jax import lax
from jax.experimental import pallas as pl
from jax.experimental.pallas import tpu as pltpu
from jax.sharding import PartitionSpec as P

K_WIN = 2


def spread_2(shard, axis, root):
    mine = lax.axis_index(axis) == root
    return lax.psum(jnp.where(mine, shard, jnp.zeros_like(shard)), axis)


def on_device_gather(
    amplitudes, slabs, couplings, occ_energy, vir_energy, occ_irrep, pair_i, pair_j, window_k, owner
):
    tile_blocks = slabs.shape[1]
    block_size = slabs.shape[3]
    block_area = block_size * block_size
    occ_count = occ_irrep.shape[0]
    local_pairs = amplitudes.shape[0]
    tile_index = lax.axis_index("vtile")
    gamma_irrep = lax.axis_index("irrep")
    beta_irreps = tile_index * tile_blocks + jnp.arange(tile_blocks, dtype=jnp.int32)
    pair_sym = jnp.bitwise_xor(occ_irrep[pair_i], occ_irrep[pair_j])
    send_index = jnp.bitwise_xor(beta_irreps[None, :], pair_sym[:, None])
    outgoing = jnp.take_along_axis(amplitudes, send_index[:, :, None], axis=1)
    local_slab = slabs[0, :, 0]
    gamma_energy = jnp.take(vir_energy, gamma_irrep, axis=0)
    beta_energy = vir_energy[beta_irreps]
    occ_keep = jnp.bitwise_xor(occ_irrep, gamma_irrep)

    def pair_term(amp_pair, occ_i, occ_j, hole_part, slab_data, k_irrep, k_energy):
        pair_irrep = jnp.bitwise_xor(occ_irrep[occ_i], occ_irrep[occ_j])
        alpha_irrep = jnp.bitwise_xor(
            jnp.bitwise_xor(pair_irrep, k_irrep), jnp.bitwise_xor(beta_irreps, gamma_irrep)
        )
        amp_sel = amp_pair[alpha_irrep].reshape(tile_blocks, block_size, block_size)
        particle = jnp.einsum(
            "mad,mdx->max", amp_sel, slab_data, preferred_element_type=jnp.float32
        )
        energy_a = vir_energy[alpha_irrep]
        base = occ_energy[occ_i] + occ_energy[occ_j] + k_energy
        denominator = (
            energy_a[:, :, None, None]
            + beta_energy[:, None, :, None]
            + gamma_energy[None, None, None, :]
            - base
        )
        triples = (
            (particle - hole_part) / denominator.reshape(tile_blocks, block_size, block_area)
        ).astype(jnp.bfloat16)
        contrib = jnp.einsum("max,mdx->mad", triples, slab_data, preferred_element_type=jnp.float32)
        return (
            jnp.zeros((8, block_area), jnp.float32)
            .at[alpha_irrep]
            .add(contrib.reshape(tile_blocks, block_area))
        )

    def coupling_rows(window, occ_j, k_irrep):
        y_column = jnp.take(couplings[window], occ_j, axis=1)
        keep_mask = jnp.bitwise_xor(occ_keep, jnp.bitwise_xor(occ_irrep[occ_j], k_irrep)) == 0
        return y_column.astype(jnp.float32) * keep_mask[:, None].astype(jnp.float32)

    empty_stash = jnp.zeros((local_pairs, occ_count, tile_blocks, block_area), jnp.bfloat16)
    empty_seen = jnp.zeros((local_pairs, occ_count), jnp.float32)
    stash = empty_stash
    seen = empty_seen
    piece_amp = lax.all_gather(outgoing, "pair", axis=0, tiled=True)
    piece_first = lax.all_gather(pair_i, "pair", axis=0, tiled=True)
    piece_second = lax.all_gather(pair_j, "pair", axis=0, tiled=True)
    match = piece_first[None, :] == pair_i[:, None]
    slot = jnp.where(match, piece_second[None, :], occ_count).astype(jnp.int32)
    row_index = jnp.broadcast_to(jnp.arange(local_pairs, dtype=jnp.int32)[:, None], slot.shape)
    spread = jnp.broadcast_to(piece_amp[None], (local_pairs,) + piece_amp.shape)
    stash = stash.at[row_index, slot].add(spread, mode="drop")
    seen = seen.at[row_index, slot].add(jnp.ones(slot.shape, jnp.float32), mode="drop")
    accumulated = jnp.zeros((local_pairs, 8, block_area), jnp.float32)
    for window in range(K_WIN):
        slab_data = spread_2(local_slab, "pair", owner[window])
        k_index = window_k[window]
        k_irrep = occ_irrep[k_index]
        k_energy = occ_energy[k_index]

        def folded_step(packed):
            amp_pair, occ_i, occ_j, slot_amp, slot_seen = packed
            coef_rows = coupling_rows(window, occ_j, k_irrep)
            coupling = (coef_rows * slot_seen[:, None]).astype(jnp.bfloat16)
            hole_part = jnp.einsum(
                "qmx,qc->mxc", slot_amp, coupling, preferred_element_type=jnp.float32
            )
            hole_part = hole_part.reshape(tile_blocks, block_size, block_area)
            return pair_term(amp_pair, occ_i, occ_j, hole_part, slab_data, k_irrep, k_energy)

        contrib_all = lax.map(folded_step, (amplitudes, pair_i, pair_j, stash, seen))
        accumulated = accumulated + contrib_all
    summed = lax.psum(accumulated, ("vtile", "irrep"))
    irrep_count = lax.axis_size("irrep")
    share = block_area // irrep_count
    summed = lax.dynamic_slice_in_dim(summed, tile_index * tile_blocks, tile_blocks, 1)
    return lax.dynamic_slice_in_dim(summed, gamma_irrep * share, share, 2)


GROUP = 16
LANE = 128
TILE = 256


def tile_plan(rows):
    lanes = -(-GROUP * rows // TILE) * TILE
    depth = LANE // GROUP
    starts = []
    for first in range(0, lanes, TILE):
        lowest = min(first // rows, GROUP - depth)
        highest = min((first + TILE - 1) // rows, GROUP - 1)
        assert lowest >= 0 and highest < lowest + depth
        starts.append(lowest)
    return lanes, depth, starts


def b_chunks(block):
    unit = LANE // math.gcd(LANE, block)
    size = 2 * unit
    return [(first, min(size, block - first)) for first in range(0, block, size)]


def triples_kernel(
    eb_ref, vt_ref, v_ref, at_ref, arep_ref, ct_ref, mask_ref, ecol_ref, lrow_ref, o_ref, t_ref, acc_ref
):
    count, block = vt_ref.shape[1], vt_ref.shape[2]
    depth = mask_ref.shape[1] // GROUP
    tiles = mask_ref.shape[0]
    window = pl.program_id(1)

    def pair_of_b(step, carry):
        for tile in range(tiles):
            lanes = slice(tile * TILE, (tile + 1) * TILE)
            top = at_ref[0, :, lanes]
            results = []
            for half in range(2):
                b = 2 * step + half
                lhs = jnp.concatenate([vt_ref[0, b], ct_ref[0, 0, tile]], axis=1)
                hole_amp = arep_ref[0, 0, b, :, lanes]
                bottom = jnp.concatenate([hole_amp] * depth, axis=0) * mask_ref[tile]
                rhs = jnp.concatenate([top, bottom], axis=0)
                numer = jnp.dot(lhs, rhs, preferred_element_type=jnp.float32)
                denom = (ecol_ref[...] + eb_ref[window, b]) + lrow_ref[0, 0, :, lanes]
                results.append(numer / denom)
            rows = pl.ds(pl.multiple_of(step * (2 * block), 2 * block), 2 * block)
            t_ref[rows, lanes] = jnp.concatenate(results, axis=0).astype(jnp.bfloat16)
        return carry

    lax.fori_loop(0, count // 2, pair_of_b, 0)
    contrib = jnp.dot(v_ref[0], t_ref[...], preferred_element_type=jnp.float32)

    @pl.when(window == 0)
    def _():
        acc_ref[...] = contrib

    @pl.when(window > 0)
    def _():
        acc_ref[...] += contrib

    @pl.when(window == pl.num_programs(1) - 1)
    def _():
        o_ref[0] = acc_ref[...].T


def triples_call(eb, vt, v, at, arep, ct, mask, ecol, lrow):
    windows, count, block, _ = vt.shape
    groups, depth_rows, lanes = at.shape
    grid = (groups, windows)
    return pl.pallas_call(
        triples_kernel,
        grid=grid,
        in_specs=[
            pl.BlockSpec(memory_space=pltpu.SMEM),
            pl.BlockSpec((1, count, block, LANE), lambda g, w: (w, 0, 0, 0)),
            pl.BlockSpec((1, block, count * block), lambda g, w: (w, 0, 0)),
            pl.BlockSpec((1, depth_rows, lanes), lambda g, w: (g, 0, 0)),
            pl.BlockSpec((1, 1, count, GROUP, lanes), lambda g, w: (w, g, 0, 0, 0)),
            pl.BlockSpec((1, 1) + ct.shape[2:], lambda g, w: (w, g, 0, 0, 0)),
            pl.BlockSpec(mask.shape, lambda g, w: (0, 0, 0)),
            pl.BlockSpec(ecol.shape, lambda g, w: (0, 0)),
            pl.BlockSpec((1, 1, 1, lanes), lambda g, w: (w, g, 0, 0)),
        ],
        out_specs=pl.BlockSpec((1, lanes, block), lambda g, w: (g, 0, 0)),
        out_shape=jax.ShapeDtypeStruct((groups, lanes, block), jnp.float32),
        scratch_shapes=[
            pltpu.VMEM((count * block, lanes), jnp.bfloat16),
            pltpu.VMEM((block, lanes), jnp.float32),
        ],
        compiler_params=pltpu.CompilerParams(
            dimension_semantics=("arbitrary", "arbitrary"), vmem_limit_bytes=48 * 1024 * 1024
        ),
        cost_estimate=pl.CostEstimate(
            flops=groups * windows * count * block * lanes * 2 * (TILE + block),
            bytes_accessed=arep.size * 2 + vt.size * 2 + v.size * 2,
            transcendentals=groups * windows * count * block * lanes,
        ),
        name="triples",
    )(eb, vt, v, at, arep, ct, mask, ecol, lrow)


def swap_cores(x):
    return lax.ppermute(x, "irrep", [(0, 1), (1, 0)])


def across(x, bit):
    count = lax.axis_size("pair")
    return lax.ppermute(x, "pair", [(t, t ^ bit) for t in range(count)])


def pick(x, index):
    return lax.dynamic_index_in_dim(x, index, 0, keepdims=False)


def fetch_slab(slab, owner, k_irrep, me, core):
    windows = owner.shape[0]
    bits = [(me >> n) & 1 for n in range(4)]
    gamma = bits[0]
    owner_bits = [[(owner[w] >> n) & 1 for n in range(4)] for w in range(windows)]
    halves = slab.reshape((2, slab.shape[0] // 2) + slab.shape[1:])
    mine, theirs = pick(halves, core), swap_cores(pick(halves, 1 - core))
    same = gamma == core
    here = jnp.where(same, mine, theirs)
    there = across(jnp.where(same, theirs, mine), 1)

    def low_block(w, high, low):
        beta = (2 * high + low) ^ (k_irrep[w] & 3) ^ gamma
        return jnp.where(owner_bits[w][0] == bits[0], pick(here, beta), pick(there, beta))

    def low_blocks(low):
        return jnp.stack([jnp.stack([low_block(w, high, low) for w in range(windows)]) for high in range(2)])

    kept = low_blocks(bits[1])
    came = across(low_blocks(1 - bits[1]), 2)
    from_here = jnp.stack([owner_bits[w][1] == bits[1] for w in range(windows)])[:, None, None]
    keep2 = jnp.where(from_here, pick(kept, bits[2]), pick(came, bits[2]))
    send2 = jnp.where(from_here, pick(kept, 1 - bits[2]), pick(came, 1 - bits[2]))
    came = across(send2, 4)
    from_here = jnp.stack([owner_bits[w][2] == bits[2] for w in range(windows)])[:, None, None]
    blocks = jnp.where(from_here, keep2, came)
    mine, theirs = pick(blocks, core), swap_cores(pick(blocks, 1 - core))
    high = (k_irrep[core] >> 2) & 1
    mine_stays = (bits[3] ^ high) == core
    kept = jnp.where(mine_stays, mine, theirs)
    came = across(jnp.where(mine_stays, theirs, mine), 8)
    block = jnp.where(((owner[core] >> 3) & 1) == bits[3], kept, came)
    other = swap_cores(block)
    return jnp.stack([jnp.where(core == 0, block, other), jnp.where(core == 0, other, block)])


def on_device_scatter(
    amplitudes, slabs, couplings, occ_energy, vir_energy, occ_irrep, pair_i, pair_j, window_k, owner
):
    betas, block = slabs.shape[1], slabs.shape[3]
    windows = window_k.shape[0]
    rows = block // lax.axis_size("irrep")
    share = rows * block
    chips = lax.axis_size("pair")
    local_pairs = pair_i.shape[0]
    pairs = chips * local_pairs
    groups = pairs // GROUP
    lanes, depth, starts = tile_plan(rows)
    me, core = lax.axis_index("pair"), lax.axis_index("irrep")
    gamma, m = me & 1, me >> 1
    k_irrep = occ_irrep[window_k]
    bf16, f32 = jnp.bfloat16, jnp.float32

    chunks = b_chunks(block)
    local = slabs[0, :, 0]
    pieces = [
        fetch_slab(local[:, :, first * block : (first + size) * block], owner, k_irrep, me, core)
        for first, size in chunks
    ]

    both = lax.all_gather(jnp.stack([pair_i, pair_j]), "pair", axis=1, tiled=True)
    numbers = jnp.arange(pairs, dtype=jnp.int32)
    ahead = both[0][None, :] < both[0][:, None]
    tied = (both[0][None, :] == both[0][:, None]) & (numbers[None, :] < numbers[:, None])
    rank = jnp.sum((ahead | tied).astype(jnp.int32), axis=1)
    placed = (rank[None, :] == numbers[:, None]).astype(jnp.int32)
    order = jnp.sum(placed * numbers[None, :], axis=1)
    first = jnp.sum(placed * both[0][None, :], axis=1)
    second = jnp.sum(placed * both[1][None, :], axis=1)

    pair_sym = occ_irrep[pair_i] ^ occ_irrep[pair_j]
    mine = lax.dynamic_slice_in_dim(amplitudes, core * share, share, 2)
    target = jnp.arange(chips, dtype=jnp.int32)
    wanted = jnp.stack([target >> 1] + [(target >> 1) ^ (target & 1) ^ k_irrep[w] for w in range(windows)], 1)
    index = wanted[:, :, None] ^ pair_sym[None, None, :]
    sent = mine[jnp.arange(local_pairs, dtype=jnp.int32)[None, None, :], index]
    kinds = 1 + windows
    came = lax.all_to_all(sent.reshape(chips, kinds * local_pairs, share), "pair", 0, 0, tiled=True)
    came = came.reshape(chips * kinds * local_pairs, share)
    source = (order // local_pairs) * (kinds * local_pairs) + order % local_pairs
    source = source[None, :] + local_pairs * jnp.arange(kinds, dtype=jnp.int32)[:, None]
    amps = came[source].reshape(kinds, groups, GROUP, rows, block)
    used = GROUP * rows
    at = amps[0].transpose(0, 3, 1, 2).reshape(groups, block, used)
    at = jnp.pad(at, ((0, 0), (0, LANE - block), (0, lanes - used)))
    lane = jnp.arange(lanes, dtype=jnp.int32)
    spread = ((lane[None, :] % rows == jnp.arange(rows)[:, None]) & (lane < used)[None, :]).astype(bf16)
    lane_pair = lane // rows
    mask = jnp.stack([
        (jnp.repeat(start + jnp.arange(depth), GROUP)[:, None] == lane_pair[None, n * TILE : (n + 1) * TILE])
        for n, start in enumerate(starts)
    ]).astype(bf16)

    coupled = jnp.where(gamma == core, couplings, swap_cores(couplings))
    chosen = (second.reshape(groups, GROUP)[:, :, None] == jnp.arange(occ_irrep.shape[0])).astype(bf16)
    coupled = jnp.einsum("gql,wljc->wgqjc", chosen, coupled)
    coupled = jnp.einsum("gpj,wgqjc->wgcpq", chosen, coupled)
    sym_j = occ_irrep[second].reshape(groups, GROUP)
    keep = (sym_j[None, :, :, None] ^ sym_j[None, :, None, :] ^ gamma ^ k_irrep[:, None, None, None]) == 0
    coupled = -(coupled * keep[:, :, None].astype(bf16))
    ct = jnp.stack(
        [coupled[:, :, :, s : s + depth].reshape(windows, groups, block, depth * GROUP) for s in starts], 2
    )

    alpha = occ_irrep[first] ^ occ_irrep[second] ^ m
    energy_a = lax.dynamic_slice_in_dim(vir_energy, core * rows, rows, 1)[alpha]
    base = occ_energy[first] + occ_energy[second]
    lrow = energy_a[None] - (base[None] + occ_energy[window_k][:, None])[:, :, None]
    lrow = lrow.reshape(windows, groups, 1, used)
    lrow = jnp.pad(lrow, ((0, 0), (0, 0), (0, 0), (0, lanes - used)), constant_values=1.0)
    ecol = jnp.broadcast_to(pick(vir_energy, gamma)[:, None], (block, TILE))
    energy_b = vir_energy[m ^ gamma ^ k_irrep]

    eye = (jnp.arange(block)[:, None] == jnp.arange(LANE)[None, :]).astype(bf16)
    total = None
    for (start, size), v in zip(chunks, pieces):
        vt = jnp.einsum("wdx,de->wxe", v, eye).reshape(windows, size, block, LANE)
        hole = amps[1:, :, :, :, start : start + size]
        arep = jnp.einsum("wgqab,ae->wgbqe", hole, spread)
        part = triples_call(energy_b[:, start : start + size], vt, v, at, arep, ct, mask, ecol, lrow)
        total = part if total is None else total + part
    total = total[:, :used].reshape(pairs, share)[rank]
    came = lax.all_to_all(total.reshape(chips, local_pairs, share), "pair", 0, 0, tiled=True)
    came = came.reshape(betas, 2, local_pairs, share)
    came = came[:, 0] + came[:, 1]
    back = jnp.arange(betas, dtype=jnp.int32)[None, :] ^ pair_sym[:, None]
    return came[back, jnp.arange(local_pairs, dtype=jnp.int32)[:, None]]


def on_device(*args):
    betas, block = args[1].shape[1], args[1].shape[3]
    chips, cores = lax.axis_size("pair"), lax.axis_size("irrep")
    fits = lax.axis_size("vtile") == 1 and cores == 2 and betas == 8 and chips == betas * cores
    if fits and args[8].shape[0] == 2 and block % 2 == 0 and block < LANE:
        return on_device_scatter(*args)
    return on_device_gather(*args)


def solution(mesh):
    placed = (
        P("pair", None, None),
        P("pair", "vtile", "irrep", None, None),
        P(None, None, None, "irrep"),
        P(),
        P(),
        P(),
        P("pair"),
        P("pair"),
        P(),
        P(),
    )
    return jax.shard_map(
        on_device,
        mesh=mesh,
        in_specs=placed,
        out_specs=P("pair", "vtile", "irrep"),
        check_vma=False,
    )
```

```python
import functools
import math

import jax
import jax.numpy as jnp
from jax import lax
from jax.experimental import pallas as pl
from jax.experimental.pallas import tpu as pltpu
from jax.sharding import PartitionSpec as P

K_WIN = 2


def spread_2(shard, axis, root):
    mine = lax.axis_index(axis) == root
    return lax.psum(jnp.where(mine, shard, jnp.zeros_like(shard)), axis)


def on_device_gather(
    amplitudes, slabs, couplings, occ_energy, vir_energy, occ_irrep, pair_i, pair_j, window_k, owner
):
    tile_blocks = slabs.shape[1]
    block_size = slabs.shape[3]
    block_area = block_size * block_size
    occ_count = occ_irrep.shape[0]
    local_pairs = amplitudes.shape[0]
    tile_index = lax.axis_index("vtile")
    gamma_irrep = lax.axis_index("irrep")
    beta_irreps = tile_index * tile_blocks + jnp.arange(tile_blocks, dtype=jnp.int32)
    pair_sym = jnp.bitwise_xor(occ_irrep[pair_i], occ_irrep[pair_j])
    send_index = jnp.bitwise_xor(beta_irreps[None, :], pair_sym[:, None])
    outgoing = jnp.take_along_axis(amplitudes, send_index[:, :, None], axis=1)
    local_slab = slabs[0, :, 0]
    gamma_energy = jnp.take(vir_energy, gamma_irrep, axis=0)
    beta_energy = vir_energy[beta_irreps]
    occ_keep = jnp.bitwise_xor(occ_irrep, gamma_irrep)

    def pair_term(amp_pair, occ_i, occ_j, hole_part, slab_data, k_irrep, k_energy):
        pair_irrep = jnp.bitwise_xor(occ_irrep[occ_i], occ_irrep[occ_j])
        alpha_irrep = jnp.bitwise_xor(
            jnp.bitwise_xor(pair_irrep, k_irrep), jnp.bitwise_xor(beta_irreps, gamma_irrep)
        )
        amp_sel = amp_pair[alpha_irrep].reshape(tile_blocks, block_size, block_size)
        particle = jnp.einsum(
            "mad,mdx->max", amp_sel, slab_data, preferred_element_type=jnp.float32
        )
        energy_a = vir_energy[alpha_irrep]
        base = occ_energy[occ_i] + occ_energy[occ_j] + k_energy
        denominator = (
            energy_a[:, :, None, None]
            + beta_energy[:, None, :, None]
            + gamma_energy[None, None, None, :]
            - base
        )
        triples = (
            (particle - hole_part) / denominator.reshape(tile_blocks, block_size, block_area)
        ).astype(jnp.bfloat16)
        contrib = jnp.einsum("max,mdx->mad", triples, slab_data, preferred_element_type=jnp.float32)
        return (
            jnp.zeros((8, block_area), jnp.float32)
            .at[alpha_irrep]
            .add(contrib.reshape(tile_blocks, block_area))
        )

    def coupling_rows(window, occ_j, k_irrep):
        y_column = jnp.take(couplings[window], occ_j, axis=1)
        keep_mask = jnp.bitwise_xor(occ_keep, jnp.bitwise_xor(occ_irrep[occ_j], k_irrep)) == 0
        return y_column.astype(jnp.float32) * keep_mask[:, None].astype(jnp.float32)

    empty_stash = jnp.zeros((local_pairs, occ_count, tile_blocks, block_area), jnp.bfloat16)
    empty_seen = jnp.zeros((local_pairs, occ_count), jnp.float32)
    stash = empty_stash
    seen = empty_seen
    piece_amp = lax.all_gather(outgoing, "pair", axis=0, tiled=True)
    piece_first = lax.all_gather(pair_i, "pair", axis=0, tiled=True)
    piece_second = lax.all_gather(pair_j, "pair", axis=0, tiled=True)
    match = piece_first[None, :] == pair_i[:, None]
    slot = jnp.where(match, piece_second[None, :], occ_count).astype(jnp.int32)
    row_index = jnp.broadcast_to(jnp.arange(local_pairs, dtype=jnp.int32)[:, None], slot.shape)
    spread = jnp.broadcast_to(piece_amp[None], (local_pairs,) + piece_amp.shape)
    stash = stash.at[row_index, slot].add(spread, mode="drop")
    seen = seen.at[row_index, slot].add(jnp.ones(slot.shape, jnp.float32), mode="drop")
    accumulated = jnp.zeros((local_pairs, 8, block_area), jnp.float32)
    for window in range(K_WIN):
        slab_data = spread_2(local_slab, "pair", owner[window])
        k_index = window_k[window]
        k_irrep = occ_irrep[k_index]
        k_energy = occ_energy[k_index]

        def folded_step(packed):
            amp_pair, occ_i, occ_j, slot_amp, slot_seen = packed
            coef_rows = coupling_rows(window, occ_j, k_irrep)
            coupling = (coef_rows * slot_seen[:, None]).astype(jnp.bfloat16)
            hole_part = jnp.einsum(
                "qmx,qc->mxc", slot_amp, coupling, preferred_element_type=jnp.float32
            )
            hole_part = hole_part.reshape(tile_blocks, block_size, block_area)
            return pair_term(amp_pair, occ_i, occ_j, hole_part, slab_data, k_irrep, k_energy)

        contrib_all = lax.map(folded_step, (amplitudes, pair_i, pair_j, stash, seen))
        accumulated = accumulated + contrib_all
    summed = lax.psum(accumulated, ("vtile", "irrep"))
    irrep_count = lax.axis_size("irrep")
    share = block_area // irrep_count
    summed = lax.dynamic_slice_in_dim(summed, tile_index * tile_blocks, tile_blocks, 1)
    return lax.dynamic_slice_in_dim(summed, gamma_irrep * share, share, 2)


GROUP = 16
LANE = 128
TILE = 256


def tile_plan(rows):
    lanes = -(-GROUP * rows // TILE) * TILE
    depth = LANE // GROUP
    starts = []
    for first in range(0, lanes, TILE):
        lowest = min(first // rows, GROUP - depth)
        highest = min((first + TILE - 1) // rows, GROUP - 1)
        assert lowest >= 0 and highest < lowest + depth
        starts.append(lowest)
    return lanes, depth, starts


def b_chunks(block):
    unit = LANE // math.gcd(LANE, block)
    size = 2 * unit
    return [(first, min(size, block - first)) for first in range(0, block, size)]


def triples_kernel(last, *refs):
    eb_ref, vt_ref, v_ref, at_ref, arep_ref, ct_ref, mask_ref, ecol_ref, lrow_ref = refs[:9]
    o_ref, t_ref = refs[-2:]
    count, block = vt_ref.shape[1], vt_ref.shape[2]
    depth = mask_ref.shape[1] // GROUP
    tiles = mask_ref.shape[0]

    def pair_of_b(step, carry):
        for tile in range(tiles):
            lanes = slice(tile * TILE, (tile + 1) * TILE)
            top = at_ref[0, :, lanes]
            results = []
            for half in range(2):
                b = 2 * step + half
                lhs = jnp.concatenate([vt_ref[0, b], ct_ref[0, 0, tile]], axis=1)
                hole_amp = arep_ref[0, 0, b, :, lanes]
                bottom = jnp.concatenate([hole_amp] * depth, axis=0) * mask_ref[tile]
                rhs = jnp.concatenate([top, bottom], axis=0)
                numer = jnp.dot(lhs, rhs, preferred_element_type=jnp.float32)
                denom = (ecol_ref[...] + eb_ref[0, b]) + lrow_ref[0, 0, :, lanes]
                results.append(numer / denom)
            rows = pl.ds(pl.multiple_of(step * (2 * block), 2 * block), 2 * block)
            t_ref[rows, lanes] = jnp.concatenate(results, axis=0).astype(jnp.bfloat16)
        return carry

    lax.fori_loop(0, count // 2, pair_of_b, 0)

    def finish(tile, carry):
        lanes = pl.ds(pl.multiple_of(tile * TILE, TILE), TILE)
        contrib = jnp.dot(v_ref[0], t_ref[:, lanes], preferred_element_type=jnp.float32)
        if len(refs) == 12:
            contrib = contrib + refs[9][0, :, lanes]
        if last:
            o_ref[0, lanes, :] = contrib.T
        else:
            o_ref[0, :, lanes] = contrib
        return carry

    lax.fori_loop(0, tiles, finish, 0)


def triples_call(window, last, eb, vt, v, at, arep, ct, mask, ecol, lrow, total=None):
    _, count, block, _ = vt.shape
    groups, depth_rows, lanes = at.shape
    w = window
    tall, wide = pl.BlockSpec((1, lanes, block), lambda g: (g, 0, 0)), pl.BlockSpec((1, block, lanes), lambda g: (g, 0, 0))
    in_specs = [
        pl.BlockSpec(memory_space=pltpu.SMEM),
        pl.BlockSpec((1, count, block, LANE), lambda g: (w, 0, 0, 0)),
        pl.BlockSpec((1, block, count * block), lambda g: (w, 0, 0)),
        pl.BlockSpec((1, depth_rows, lanes), lambda g: (g, 0, 0)),
        pl.BlockSpec((1, 1, count, GROUP, lanes), lambda g: (w, g, 0, 0, 0)),
        pl.BlockSpec((1, 1) + ct.shape[2:], lambda g: (w, g, 0, 0, 0)),
        pl.BlockSpec(mask.shape, lambda g: (0, 0, 0)),
        pl.BlockSpec(ecol.shape, lambda g: (0, 0)),
        pl.BlockSpec((1, 1, 1, lanes), lambda g: (w, g, 0, 0)),
    ]
    operands = [eb[w : w + 1], vt, v, at, arep, ct, mask, ecol, lrow]
    if total is not None:
        in_specs.append(wide)
        operands.append(total)
    shape = (groups, lanes, block) if last else (groups, block, lanes)
    return pl.pallas_call(
        functools.partial(triples_kernel, last),
        grid=(groups,),
        in_specs=in_specs,
        out_specs=tall if last else wide,
        out_shape=jax.ShapeDtypeStruct(shape, jnp.float32),
        scratch_shapes=[pltpu.VMEM((count * block, lanes), jnp.bfloat16)],
        compiler_params=pltpu.CompilerParams(
            dimension_semantics=("arbitrary",), vmem_limit_bytes=40 * 1024 * 1024
        ),
        cost_estimate=pl.CostEstimate(
            flops=groups * count * block * lanes * 2 * (TILE + block) * 4,
            bytes_accessed=(arep.size + vt.size + v.size) * 2,
            transcendentals=groups * count * block * lanes,
        ),
        name="triples",
    )(*operands)


def swap_cores(x):
    return lax.ppermute(x, "irrep", [(0, 1), (1, 0)])


def across(x, bit):
    count = lax.axis_size("pair")
    return lax.ppermute(x, "pair", [(t, t ^ bit) for t in range(count)])


def pick(x, index):
    return lax.dynamic_index_in_dim(x, index, 0, keepdims=False)


def after(x, *others):
    return lax.optimization_barrier((x,) + others)[0]


class SlabPath:
    def __init__(self, owner, k_irrep, me, core):
        self.owner, self.k_irrep, self.core = owner, k_irrep, core
        self.windows = owner.shape[0]
        self.bits = [(me >> n) & 1 for n in range(4)]

    def from_here(self, bit):
        return ((self.owner >> bit) & 1) == self.bits[bit]

    def split_cores(self, slab):
        halves = slab.reshape((2, slab.shape[0] // 2) + slab.shape[1:])
        mine, theirs = pick(halves, self.core), swap_cores(pick(halves, 1 - self.core))
        same = self.bits[0] == self.core
        return jnp.where(same, mine, theirs), jnp.where(same, theirs, mine)

    def split_low(self, kept, came):
        def block(w, high, low):
            beta = (2 * high + low) ^ (self.k_irrep[w] & 3) ^ self.bits[0]
            return jnp.where(self.from_here(0)[w], pick(kept, beta), pick(came, beta))

        def blocks(low):
            return jnp.stack(
                [jnp.stack([block(w, high, low) for w in range(self.windows)]) for high in range(2)]
            )

        return blocks(self.bits[1]), blocks(1 - self.bits[1])

    def split_high(self, kept, came):
        here = self.from_here(1)[:, None, None]
        kept, leaving = [
            jnp.where(here, pick(kept, high), pick(came, high)) for high in (self.bits[2], 1 - self.bits[2])
        ]
        return kept, leaving

    def split_top(self, kept, came):
        blocks = jnp.where(self.from_here(2)[:, None, None], kept, came)
        mine, theirs = pick(blocks, self.core), swap_cores(pick(blocks, 1 - self.core))
        stays = (self.bits[3] ^ ((self.k_irrep[self.core] >> 2) & 1)) == self.core
        return jnp.where(stays, mine, theirs), jnp.where(stays, theirs, mine)

    def join(self, kept, came):
        block = jnp.where(self.from_here(3)[self.core], kept, came)
        other = swap_cores(block)
        first = self.core == 0
        return jnp.stack([jnp.where(first, block, other), jnp.where(first, other, block)])


def on_device_scatter(
    amplitudes, slabs, couplings, occ_energy, vir_energy, occ_irrep, pair_i, pair_j, window_k, owner
):
    betas, block = slabs.shape[1], slabs.shape[3]
    windows = window_k.shape[0]
    rows = block // lax.axis_size("irrep")
    share = rows * block
    chips = lax.axis_size("pair")
    local_pairs = pair_i.shape[0]
    pairs = chips * local_pairs
    groups = pairs // GROUP
    lanes, depth, starts = tile_plan(rows)
    me, core = lax.axis_index("pair"), lax.axis_index("irrep")
    gamma, m = me & 1, me >> 1
    k_irrep = occ_irrep[window_k]
    bf16, f32 = jnp.bfloat16, jnp.float32

    chunks = b_chunks(block)
    local = slabs[0, :, 0]
    path = SlabPath(owner, k_irrep, me, core)
    kept_x, sent_x = zip(
        *[path.split_cores(local[:, :, first * block : (first + size) * block]) for first, size in chunks]
    )
    x = []
    for leaving in sent_x:
        x.append(across(after(leaving, x[-1]) if x else leaving, 1))
    kept_y, sent_y = [list(v) for v in zip(*map(path.split_low, kept_x, x))]
    y = [across(leaving, 2) for leaving in sent_y]

    pair_sym = occ_irrep[pair_i] ^ occ_irrep[pair_j]
    mine = lax.dynamic_slice_in_dim(amplitudes, core * share, share, 2)
    target = jnp.arange(chips, dtype=jnp.int32)
    wanted = jnp.stack([target >> 1] + [(target >> 1) ^ (target & 1) ^ k_irrep[w] for w in range(windows)], 1)
    index = wanted[:, :, None] ^ pair_sym[None, None, :]
    sent = mine[jnp.arange(local_pairs, dtype=jnp.int32)[None, None, :], index]
    kinds = 1 + windows
    sent = sent.reshape(chips, kinds * local_pairs, share)
    labels = jnp.concatenate([pair_i, pair_j]).astype(bf16)
    labels = jnp.pad(labels, (0, share - labels.shape[0]))
    sent = jnp.concatenate([sent, jnp.broadcast_to(labels, (chips, 1, share))], 1)
    came = lax.all_to_all(after(sent, sent_x[0]), "pair", 0, 0, tiled=True)
    came = after(came, sent_y[0])
    both = came[:, -1, : 2 * local_pairs].astype(jnp.int32).reshape(chips, 2, local_pairs)
    both = both.transpose(1, 0, 2).reshape(2, pairs)

    numbers = jnp.arange(pairs, dtype=jnp.int32)
    ahead = both[0][None, :] < both[0][:, None]
    tied = (both[0][None, :] == both[0][:, None]) & (numbers[None, :] < numbers[:, None])
    rank = jnp.sum((ahead | tied).astype(jnp.int32), axis=1)
    placed = (rank[None, :] == numbers[:, None]).astype(jnp.int32)
    order = jnp.sum(placed * numbers[None, :], axis=1)
    first = jnp.sum(placed * both[0][None, :], axis=1)
    second = jnp.sum(placed * both[1][None, :], axis=1)

    came = came.reshape(chips * (kinds * local_pairs + 1), share)
    source = (order // local_pairs) * (kinds * local_pairs + 1) + order % local_pairs
    source = source[None, :] + local_pairs * jnp.arange(kinds, dtype=jnp.int32)[:, None]
    amps = came[source].reshape(kinds, groups, GROUP, rows, block)
    used = GROUP * rows
    at = amps[0].transpose(0, 3, 1, 2).reshape(groups, block, used)
    at = jnp.pad(at, ((0, 0), (0, LANE - block), (0, lanes - used)))
    lane = jnp.arange(lanes, dtype=jnp.int32)
    spread = ((lane[None, :] % rows == jnp.arange(rows)[:, None]) & (lane < used)[None, :]).astype(bf16)
    lane_pair = lane // rows
    mask = jnp.stack([
        (jnp.repeat(start + jnp.arange(depth), GROUP)[:, None] == lane_pair[None, n * TILE : (n + 1) * TILE])
        for n, start in enumerate(starts)
    ]).astype(bf16)

    coupled = jnp.where(gamma == core, couplings, swap_cores(couplings))
    chosen = (second.reshape(groups, GROUP)[:, :, None] == jnp.arange(occ_irrep.shape[0])).astype(bf16)
    coupled = jnp.einsum("gql,wljc->wgqjc", chosen, coupled)
    coupled = jnp.einsum("gpj,wgqjc->wgcpq", chosen, coupled)
    sym_j = occ_irrep[second].reshape(groups, GROUP)
    keep = (sym_j[None, :, :, None] ^ sym_j[None, :, None, :] ^ gamma ^ k_irrep[:, None, None, None]) == 0
    coupled = -(coupled * keep[:, :, None].astype(bf16))
    ct = jnp.stack(
        [coupled[:, :, :, s : s + depth].reshape(windows, groups, block, depth * GROUP) for s in starts], 2
    )

    alpha = occ_irrep[first] ^ occ_irrep[second] ^ m
    energy_a = lax.dynamic_slice_in_dim(vir_energy, core * rows, rows, 1)[alpha]
    base = occ_energy[first] + occ_energy[second]
    lrow = energy_a[None] - (base[None] + occ_energy[window_k][:, None])[:, :, None]
    lrow = lrow.reshape(windows, groups, 1, used)
    lrow = jnp.pad(lrow, ((0, 0), (0, 0), (0, 0), (0, lanes - used)), constant_values=1.0)
    ecol = jnp.broadcast_to(pick(vir_energy, gamma)[:, None], (block, TILE))
    energy_b = vir_energy[m ^ gamma ^ k_irrep]

    eye = (jnp.arange(block)[:, None] == jnp.arange(LANE)[None, :]).astype(bf16)
    areps = [
        jnp.einsum("wgqab,ae->wgbqe", amps[1:, :, :, :, start : start + size], spread) for start, size in chunks
    ]

    def run(chunk, w, v, total):
        start, size = chunks[chunk]
        vt = jnp.einsum("wdx,de->wxe", v, eye).reshape(windows, size, block, LANE)
        last = start + size == block and w == windows - 1
        energies = energy_b[:, start : start + size]
        return triples_call(w, last, energies, vt, v, at, areps[chunk], ct, mask, ecol, lrow, total)

    calls = [(chunk, w) for chunk in range(len(chunks)) for w in range(windows)]
    kept_z, sent_z, kept_h, sent_h, z, h, ready = {}, {}, {}, {}, {}, {}, {}

    def to_high(chunk, token=None):
        came_y = y[chunk] if token is None else after(y[chunk], token)
        kept_z[chunk], sent_z[chunk] = path.split_high(kept_y[chunk], came_y)
        z[chunk] = across(sent_z[chunk], 4)
        return sent_z[chunk]

    def to_top(chunk, token=None):
        came_z = z[chunk] if token is None else after(z[chunk], token)
        kept_h[chunk], sent_h[chunk] = path.split_top(kept_z[chunk], came_z)
        h[chunk] = across(sent_h[chunk], 8)
        return sent_h[chunk]

    def arrive(chunk, token=None):
        came_h = h[chunk] if token is None else after(h[chunk], token)
        ready[chunk] = path.join(kept_h[chunk], came_h)
        return ready[chunk]

    plan = {0: [(to_top, 1), (to_high, 2)], 1: [(arrive, 1), (to_top, 2)], 2: [(arrive, 2)]}
    to_high(0)
    to_top(0)
    arrive(0)
    ready[0] = after(ready[0], to_high(1), sent_y[2])
    total = None
    for n, (chunk, w) in enumerate(calls):
        total = run(chunk, w, ready[chunk], total)
        issued = [move(number, total) for move, number in plan.get(n, [])]
        if issued:
            total = after(total, *issued)
    total = total[:, :used].reshape(pairs, share)[rank]
    came = lax.all_to_all(total.reshape(chips, local_pairs, share), "pair", 0, 0, tiled=True)
    came = came.reshape(betas, 2, local_pairs, share)
    came = came[:, 0] + came[:, 1]
    back = jnp.arange(betas, dtype=jnp.int32)[None, :] ^ pair_sym[:, None]
    return came[back, jnp.arange(local_pairs, dtype=jnp.int32)[:, None]]


def on_device(*args):
    betas, block = args[1].shape[1], args[1].shape[3]
    chips, cores = lax.axis_size("pair"), lax.axis_size("irrep")
    fits = lax.axis_size("vtile") == 1 and cores == 2 and betas == 8 and chips == betas * cores
    fits = fits and args[8].shape[0] == 2 and block % 2 == 0 and block < LANE
    if fits and args[5].shape[0] <= 256:
        return on_device_scatter(*args)
    return on_device_gather(*args)


def solution(mesh):
    placed = (
        P("pair", None, None),
        P("pair", "vtile", "irrep", None, None),
        P(None, None, None, "irrep"),
        P(),
        P(),
        P(),
        P("pair"),
        P("pair"),
        P(),
        P(),
    )
    return jax.shard_map(
        on_device,
        mesh=mesh,
        in_specs=placed,
        out_specs=P("pair", "vtile", "irrep"),
        check_vma=False,
    )
```

```python
import functools
import math

import jax
import jax.numpy as jnp
from jax import lax
from jax.experimental import pallas as pl
from jax.experimental.pallas import tpu as pltpu
from jax.sharding import PartitionSpec as P


K_WIN = 2


def spread_2(shard, axis, root):
    mine = lax.axis_index(axis) == root
    return lax.psum(jnp.where(mine, shard, jnp.zeros_like(shard)), axis)


def on_device_gather(
    amplitudes, slabs, couplings, occ_energy, vir_energy, occ_irrep, pair_i, pair_j, window_k, owner
):
    tile_blocks = slabs.shape[1]
    block_size = slabs.shape[3]
    block_area = block_size * block_size
    occ_count = occ_irrep.shape[0]
    local_pairs = amplitudes.shape[0]
    tile_index = lax.axis_index("vtile")
    gamma_irrep = lax.axis_index("irrep")
    beta_irreps = tile_index * tile_blocks + jnp.arange(tile_blocks, dtype=jnp.int32)
    pair_sym = jnp.bitwise_xor(occ_irrep[pair_i], occ_irrep[pair_j])
    send_index = jnp.bitwise_xor(beta_irreps[None, :], pair_sym[:, None])
    outgoing = jnp.take_along_axis(amplitudes, send_index[:, :, None], axis=1)
    local_slab = slabs[0, :, 0]
    gamma_energy = jnp.take(vir_energy, gamma_irrep, axis=0)
    beta_energy = vir_energy[beta_irreps]
    occ_keep = jnp.bitwise_xor(occ_irrep, gamma_irrep)

    def pair_term(amp_pair, occ_i, occ_j, hole_part, slab_data, k_irrep, k_energy):
        pair_irrep = jnp.bitwise_xor(occ_irrep[occ_i], occ_irrep[occ_j])
        alpha_irrep = jnp.bitwise_xor(
            jnp.bitwise_xor(pair_irrep, k_irrep), jnp.bitwise_xor(beta_irreps, gamma_irrep)
        )
        amp_sel = amp_pair[alpha_irrep].reshape(tile_blocks, block_size, block_size)
        particle = jnp.einsum(
            "mad,mdx->max", amp_sel, slab_data, preferred_element_type=jnp.float32
        )
        energy_a = vir_energy[alpha_irrep]
        base = occ_energy[occ_i] + occ_energy[occ_j] + k_energy
        denominator = (
            energy_a[:, :, None, None]
            + beta_energy[:, None, :, None]
            + gamma_energy[None, None, None, :]
            - base
        )
        triples = (
            (particle - hole_part) / denominator.reshape(tile_blocks, block_size, block_area)
        ).astype(jnp.bfloat16)
        contrib = jnp.einsum("max,mdx->mad", triples, slab_data, preferred_element_type=jnp.float32)
        return (
            jnp.zeros((8, block_area), jnp.float32)
            .at[alpha_irrep]
            .add(contrib.reshape(tile_blocks, block_area))
        )

    def coupling_rows(window, occ_j, k_irrep):
        y_column = jnp.take(couplings[window], occ_j, axis=1)
        keep_mask = jnp.bitwise_xor(occ_keep, jnp.bitwise_xor(occ_irrep[occ_j], k_irrep)) == 0
        return y_column.astype(jnp.float32) * keep_mask[:, None].astype(jnp.float32)

    empty_stash = jnp.zeros((local_pairs, occ_count, tile_blocks, block_area), jnp.bfloat16)
    empty_seen = jnp.zeros((local_pairs, occ_count), jnp.float32)
    stash = empty_stash
    seen = empty_seen
    piece_amp = lax.all_gather(outgoing, "pair", axis=0, tiled=True)
    piece_first = lax.all_gather(pair_i, "pair", axis=0, tiled=True)
    piece_second = lax.all_gather(pair_j, "pair", axis=0, tiled=True)
    match = piece_first[None, :] == pair_i[:, None]
    slot = jnp.where(match, piece_second[None, :], occ_count).astype(jnp.int32)
    row_index = jnp.broadcast_to(jnp.arange(local_pairs, dtype=jnp.int32)[:, None], slot.shape)
    spread = jnp.broadcast_to(piece_amp[None], (local_pairs,) + piece_amp.shape)
    stash = stash.at[row_index, slot].add(spread, mode="drop")
    seen = seen.at[row_index, slot].add(jnp.ones(slot.shape, jnp.float32), mode="drop")
    accumulated = jnp.zeros((local_pairs, 8, block_area), jnp.float32)
    for window in range(K_WIN):
        slab_data = spread_2(local_slab, "pair", owner[window])
        k_index = window_k[window]
        k_irrep = occ_irrep[k_index]
        k_energy = occ_energy[k_index]

        def folded_step(packed):
            amp_pair, occ_i, occ_j, slot_amp, slot_seen = packed
            coef_rows = coupling_rows(window, occ_j, k_irrep)
            coupling = (coef_rows * slot_seen[:, None]).astype(jnp.bfloat16)
            hole_part = jnp.einsum(
                "qmx,qc->mxc", slot_amp, coupling, preferred_element_type=jnp.float32
            )
            hole_part = hole_part.reshape(tile_blocks, block_size, block_area)
            return pair_term(amp_pair, occ_i, occ_j, hole_part, slab_data, k_irrep, k_energy)

        contrib_all = lax.map(folded_step, (amplitudes, pair_i, pair_j, stash, seen))
        accumulated = accumulated + contrib_all
    summed = lax.psum(accumulated, ("vtile", "irrep"))
    irrep_count = lax.axis_size("irrep")
    share = block_area // irrep_count
    summed = lax.dynamic_slice_in_dim(summed, tile_index * tile_blocks, tile_blocks, 1)
    return lax.dynamic_slice_in_dim(summed, gamma_irrep * share, share, 2)


GROUP = 16
LANE = 128
TILE = 256


def tile_plan(rows):
    lanes = -(-GROUP * rows // TILE) * TILE
    depth = LANE // GROUP
    starts = []
    for first in range(0, lanes, TILE):
        lowest = min(first // rows, GROUP - depth)
        highest = min((first + TILE - 1) // rows, GROUP - 1)
        assert lowest >= 0 and highest < lowest + depth
        starts.append(lowest)
    return lanes, depth, starts


def b_chunks(block):
    unit = LANE // math.gcd(LANE, block)
    size = 2 * unit
    return [(first, min(size, block - first)) for first in range(0, block, size)]


def triples_kernel(last, *refs):
    eb_ref, vt_ref, v_ref, at_ref, arep_ref, ct_ref, mask_ref, ecol_ref, lrow_ref = refs[:9]
    o_ref, t_ref = refs[-2:]
    count, block = vt_ref.shape[1], vt_ref.shape[2]
    depth = mask_ref.shape[1] // GROUP
    tiles = mask_ref.shape[0]

    def pair_of_b(step, carry):
        for tile in range(tiles):
            lanes = slice(tile * TILE, (tile + 1) * TILE)
            top = at_ref[0, :, lanes]
            results = []
            for half in range(2):
                b = 2 * step + half
                lhs = jnp.concatenate([vt_ref[0, b], ct_ref[0, 0, tile]], axis=1)
                hole_amp = arep_ref[0, 0, b, :, lanes]
                bottom = jnp.concatenate([hole_amp] * depth, axis=0) * mask_ref[tile]
                rhs = jnp.concatenate([top, bottom], axis=0)
                numer = jnp.dot(lhs, rhs, preferred_element_type=jnp.float32)
                denom = (ecol_ref[...] + eb_ref[0, b]) + lrow_ref[0, 0, :, lanes]
                results.append(numer / denom)
            rows = pl.ds(pl.multiple_of(step * (2 * block), 2 * block), 2 * block)
            t_ref[rows, lanes] = jnp.concatenate(results, axis=0).astype(jnp.bfloat16)
        return carry

    lax.fori_loop(0, count // 2, pair_of_b, 0)

    def finish(tile, carry):
        lanes = pl.ds(pl.multiple_of(tile * TILE, TILE), TILE)
        contrib = jnp.dot(v_ref[0], t_ref[:, lanes], preferred_element_type=jnp.float32)
        if len(refs) == 12:
            contrib = contrib + refs[9][0, :, lanes]
        if last:
            o_ref[0, lanes, :] = contrib.T
        else:
            o_ref[0, :, lanes] = contrib
        return carry

    lax.fori_loop(0, tiles, finish, 0)


def triples_call(window, last, eb, vt, v, at, arep, ct, mask, ecol, lrow, total=None):
    _, count, block, _ = vt.shape
    groups, depth_rows, lanes = at.shape
    w = window
    tall, wide = pl.BlockSpec((1, lanes, block), lambda g: (g, 0, 0)), pl.BlockSpec((1, block, lanes), lambda g: (g, 0, 0))
    in_specs = [
        pl.BlockSpec(memory_space=pltpu.SMEM),
        pl.BlockSpec((1, count, block, LANE), lambda g: (w, 0, 0, 0)),
        pl.BlockSpec((1, block, count * block), lambda g: (w, 0, 0)),
        pl.BlockSpec((1, depth_rows, lanes), lambda g: (g, 0, 0)),
        pl.BlockSpec((1, 1, count, GROUP, lanes), lambda g: (w, g, 0, 0, 0)),
        pl.BlockSpec((1, 1) + ct.shape[2:], lambda g: (w, g, 0, 0, 0)),
        pl.BlockSpec(mask.shape, lambda g: (0, 0, 0)),
        pl.BlockSpec(ecol.shape, lambda g: (0, 0)),
        pl.BlockSpec((1, 1, 1, lanes), lambda g: (w, g, 0, 0)),
    ]
    operands = [eb[w : w + 1], vt, v, at, arep, ct, mask, ecol, lrow]
    if total is not None:
        in_specs.append(wide)
        operands.append(total)
    shape = (groups, lanes, block) if last else (groups, block, lanes)
    return pl.pallas_call(
        functools.partial(triples_kernel, last),
        grid=(groups,),
        in_specs=in_specs,
        out_specs=tall if last else wide,
        out_shape=jax.ShapeDtypeStruct(shape, jnp.float32),
        scratch_shapes=[pltpu.VMEM((count * block, lanes), jnp.bfloat16)],
        compiler_params=pltpu.CompilerParams(
            dimension_semantics=("arbitrary",), vmem_limit_bytes=40 * 1024 * 1024
        ),
        cost_estimate=pl.CostEstimate(
            flops=groups * count * block * lanes * 2 * (TILE + block) * 4,
            bytes_accessed=(arep.size + vt.size + v.size) * 2,
            transcendentals=groups * count * block * lanes,
        ),
        name="triples",
    )(*operands)


def swap_cores(x):
    return lax.ppermute(x, "irrep", [(0, 1), (1, 0)])


def across(x, bit):
    count = lax.axis_size("pair")
    return lax.ppermute(x, "pair", [(t, t ^ bit) for t in range(count)])


def pick(x, index):
    return lax.dynamic_index_in_dim(x, index, 0, keepdims=False)


def after(x, *others):
    return lax.optimization_barrier((x,) + others)[0]


class SlabPath:
    def __init__(self, owner, k_irrep, me, core):
        self.owner, self.k_irrep, self.core = owner, k_irrep, core
        self.windows = owner.shape[0]
        self.bits = [(me >> n) & 1 for n in range(4)]

    def from_here(self, bit):
        return ((self.owner >> bit) & 1) == self.bits[bit]

    def split_cores(self, slab):
        halves = slab.reshape((2, slab.shape[0] // 2) + slab.shape[1:])
        mine, theirs = pick(halves, self.core), swap_cores(pick(halves, 1 - self.core))
        same = self.bits[0] == self.core
        return jnp.where(same, mine, theirs), jnp.where(same, theirs, mine)

    def split_low(self, kept, came):
        def block(w, high, low):
            beta = (2 * high + low) ^ (self.k_irrep[w] & 3) ^ self.bits[0]
            return jnp.where(self.from_here(0)[w], pick(kept, beta), pick(came, beta))

        def blocks(low):
            return jnp.stack(
                [jnp.stack([block(w, high, low) for w in range(self.windows)]) for high in range(2)]
            )

        return blocks(self.bits[1]), blocks(1 - self.bits[1])

    def split_high(self, kept, came):
        here = self.from_here(1)[:, None, None]
        kept, leaving = [
            jnp.where(here, pick(kept, high), pick(came, high)) for high in (self.bits[2], 1 - self.bits[2])
        ]
        return kept, leaving

    def split_top(self, kept, came):
        blocks = jnp.where(self.from_here(2)[:, None, None], kept, came)
        mine, theirs = pick(blocks, self.core), swap_cores(pick(blocks, 1 - self.core))
        stays = (self.bits[3] ^ ((self.k_irrep[self.core] >> 2) & 1)) == self.core
        return jnp.where(stays, mine, theirs), jnp.where(stays, theirs, mine)

    def join(self, kept, came):
        block = jnp.where(self.from_here(3)[self.core], kept, came)
        other = swap_cores(block)
        first = self.core == 0
        return jnp.stack([jnp.where(first, block, other), jnp.where(first, other, block)])


def on_device_scatter(
    amplitudes, slabs, couplings, occ_energy, vir_energy, occ_irrep, pair_i, pair_j, window_k, owner
):
    betas, block = slabs.shape[1], slabs.shape[3]
    windows = window_k.shape[0]
    rows = block // lax.axis_size("irrep")
    share = rows * block
    chips = lax.axis_size("pair")
    local_pairs = pair_i.shape[0]
    pairs = chips * local_pairs
    groups = pairs // GROUP
    lanes, depth, starts = tile_plan(rows)
    me, core = lax.axis_index("pair"), lax.axis_index("irrep")
    gamma, m = me & 1, me >> 1
    k_irrep = occ_irrep[window_k]
    bf16 = jnp.bfloat16

    chunks = b_chunks(block)
    local = slabs[0, :, 0]
    path = SlabPath(owner, k_irrep, me, core)
    kept_x, sent_x = zip(
        *[path.split_cores(local[:, :, first * block : (first + size) * block]) for first, size in chunks]
    )
    x, leaving_x = [], []
    for leaving in sent_x:
        leaving_x.append(after(leaving, x[-1]) if x else leaving)
        x.append(across(leaving_x[-1], 1))
    kept_y, sent_y = [], []
    for kept, came in zip(kept_x, x):
        kept, leaving = path.split_low(kept, after(came, sent_y[-1]) if sent_y else came)
        kept_y.append(kept)
        sent_y.append(leaving)
    y = [across(leaving, 2) for leaving in sent_y]

    pair_sym = occ_irrep[pair_i] ^ occ_irrep[pair_j]
    mine = lax.dynamic_slice_in_dim(after(amplitudes, sent_x[0]), core * share, share, 2)
    target = jnp.arange(chips, dtype=jnp.int32)
    wanted = jnp.stack([target >> 1] + [(target >> 1) ^ (target & 1) ^ k_irrep[w] for w in range(windows)], 1)
    index = wanted[:, :, None] ^ pair_sym[None, None, :]
    sent = mine[jnp.arange(local_pairs, dtype=jnp.int32)[None, None, :], index]
    kinds = 1 + windows
    sent = sent.reshape(chips, kinds * local_pairs, share)
    labels = jnp.concatenate([pair_i, pair_j]).astype(bf16)
    labels = jnp.pad(labels, (0, share - labels.shape[0]))
    sent = jnp.concatenate([sent, jnp.broadcast_to(labels, (chips, 1, share))], 1)
    came = lax.all_to_all(sent, "pair", 0, 0, tiled=True)
    came = after(came, sent_y[0], leaving_x[1])
    came = came.reshape(chips * (kinds * local_pairs + 1), share)
    label_rows = after(target, leaving_x[1]) * (kinds * local_pairs + 1) + kinds * local_pairs
    both = came[label_rows][:, : 2 * local_pairs].astype(jnp.int32).reshape(chips, 2, local_pairs)
    both = both.transpose(1, 0, 2).reshape(2, pairs)

    numbers = jnp.arange(pairs, dtype=jnp.int32)
    ahead = both[0][None, :] < both[0][:, None]
    tied = (both[0][None, :] == both[0][:, None]) & (numbers[None, :] < numbers[:, None])
    rank = jnp.sum((ahead | tied).astype(jnp.int32), axis=1)
    placed = (rank[None, :] == numbers[:, None]).astype(jnp.int32)
    order = jnp.sum(placed * numbers[None, :], axis=1)
    first = jnp.sum(placed * both[0][None, :], axis=1)
    second = jnp.sum(placed * both[1][None, :], axis=1)

    source = (order // local_pairs) * (kinds * local_pairs + 1) + order % local_pairs
    source = source[None, :] + local_pairs * jnp.arange(kinds, dtype=jnp.int32)[:, None]
    amps = came[source]
    amps = amps.reshape(kinds, groups, GROUP, rows, block)
    holes = amps[1:]
    used = GROUP * rows
    at = amps[0].transpose(0, 3, 1, 2).reshape(groups, block, used)
    at = jnp.pad(at, ((0, 0), (0, LANE - block), (0, lanes - used)))
    lane = jnp.arange(lanes, dtype=jnp.int32)
    spread = ((lane[None, :] % rows == jnp.arange(rows)[:, None]) & (lane < used)[None, :]).astype(bf16)
    lane_pair = lane // rows
    mask = jnp.stack([
        (jnp.repeat(start + jnp.arange(depth), GROUP)[:, None] == lane_pair[None, n * TILE : (n + 1) * TILE])
        for n, start in enumerate(starts)
    ]).astype(bf16)

    coupled = jnp.where(gamma == core, couplings, swap_cores(couplings))
    chosen = (second.reshape(groups, GROUP)[:, :, None] == jnp.arange(occ_irrep.shape[0])).astype(bf16)
    coupled = jnp.einsum("gql,wljc->wgqjc", chosen, coupled)
    coupled = jnp.einsum("gpj,wgqjc->wgcpq", chosen, coupled)
    sym_j = occ_irrep[second].reshape(groups, GROUP)
    keep = (sym_j[None, :, :, None] ^ sym_j[None, :, None, :] ^ gamma ^ k_irrep[:, None, None, None]) == 0
    coupled = -(coupled * keep[:, :, None].astype(bf16))
    ct = jnp.stack(
        [coupled[:, :, :, s : s + depth].reshape(windows, groups, block, depth * GROUP) for s in starts], 2
    )

    alpha = occ_irrep[first] ^ occ_irrep[second] ^ m
    energy_a = lax.dynamic_slice_in_dim(vir_energy, core * rows, rows, 1)[alpha]
    base = occ_energy[first] + occ_energy[second]
    lrow = energy_a[None] - (base[None] + occ_energy[window_k][:, None])[:, :, None]
    lrow = lrow.reshape(windows, groups, 1, used)
    lrow = jnp.pad(lrow, ((0, 0), (0, 0), (0, 0), (0, lanes - used)), constant_values=1.0)
    ecol = jnp.broadcast_to(pick(vir_energy, gamma)[:, None], (block, TILE))
    energy_b = vir_energy[m ^ gamma ^ k_irrep]

    eye = (jnp.arange(block)[:, None] == jnp.arange(LANE)[None, :]).astype(bf16)

    def spread_holes(chunk, *tokens):
        start, size = chunks[chunk]
        hole = after(holes[:, :, :, :, start : start + size], *tokens)
        return jnp.einsum("wgqab,ae->wgbqe", hole, spread)

    def run(chunk, w, v, total):
        start, size = chunks[chunk]
        vt = jnp.einsum("wdx,de->wxe", v, eye).reshape(windows, size, block, LANE)
        last = start + size == block and w == windows - 1
        energies = energy_b[:, start : start + size]
        return triples_call(w, last, energies, vt, v, at, areps[chunk], ct, mask, ecol, lrow, total)

    calls = [(chunk, w) for chunk in range(len(chunks)) for w in range(windows)]
    kept_z, sent_z, kept_h, sent_h, z, h, ready = {}, {}, {}, {}, {}, {}, {}

    def to_high(chunk, token=None):
        came_y = y[chunk] if token is None else after(y[chunk], token)
        kept_z[chunk], sent_z[chunk] = path.split_high(kept_y[chunk], came_y)
        z[chunk] = across(sent_z[chunk], 4)
        return sent_z[chunk]

    def to_top(chunk, token=None):
        came_z = z[chunk] if token is None else after(z[chunk], token)
        kept_h[chunk], sent_h[chunk] = path.split_top(kept_z[chunk], came_z)
        h[chunk] = across(sent_h[chunk], 8)
        return sent_h[chunk]

    def arrive(chunk, token=None):
        came_h = h[chunk] if token is None else after(h[chunk], token)
        ready[chunk] = path.join(kept_h[chunk], came_h)
        return ready[chunk]

    plan = {0: [(to_top, 1), (to_high, 2)], 1: [(arrive, 1), (to_top, 2)], 2: [(arrive, 2)]}
    to_high(0, amps)
    at = after(at, sent_z[0], sent_y[1], leaving_x[2])
    areps = [spread_holes(0, at)]
    to_top(0, areps[0])
    ct = after(ct, sent_h[0])
    arrive(0, ct)
    ready[0] = after(ready[0], to_high(1, sent_h[0]), sent_y[2])
    total = None
    for n, (chunk, w) in enumerate(calls):
        total = run(chunk, w, ready[chunk], total)
        issued = [move(number, total) for move, number in plan.get(n, [])]
        if n == 0:
            areps += [spread_holes(number, total) for number in range(1, len(chunks))]
        if issued:
            total = after(total, *issued)
    total = total[:, :used].reshape(pairs, share)[rank]
    cut = 8 if share % 8 == 0 else 1
    total = total.reshape(chips, local_pairs * cut, share // cut)
    came = lax.all_to_all(total, "pair", 0, 0, tiled=True)
    came = came.reshape(betas, 2, local_pairs, cut, share // cut)
    came = (came[:, 0] + came[:, 1]).reshape(betas, local_pairs, share)
    back = jnp.arange(betas, dtype=jnp.int32)[None, :] ^ pair_sym[:, None]
    return came[back, jnp.arange(local_pairs, dtype=jnp.int32)[:, None]]


def on_device(*args):
    betas, block = args[1].shape[1], args[1].shape[3]
    chips, cores = lax.axis_size("pair"), lax.axis_size("irrep")
    fits = lax.axis_size("vtile") == 1 and cores == 2 and betas == 8 and chips == betas * cores
    fits = fits and args[8].shape[0] == 2 and block % 2 == 0 and block < LANE
    if fits and args[5].shape[0] <= 256:
        return on_device_scatter(*args)
    return on_device_gather(*args)


def solution(mesh):
    placed = (
        P("pair", None, None),
        P("pair", "vtile", "irrep", None, None),
        P(None, None, None, "irrep"),
        P(),
        P(),
        P(),
        P("pair"),
        P("pair"),
        P(),
        P(),
    )
    return jax.shard_map(
        on_device,
        mesh=mesh,
        in_specs=placed,
        out_specs=P("pair", "vtile", "irrep"),
        check_vma=False,
    )
```

```python
import functools
import math

import jax
import jax.numpy as jnp
from jax import lax
from jax.experimental import pallas as pl
from jax.experimental.pallas import tpu as pltpu
from jax.sharding import PartitionSpec as P


K_WIN = 2


def spread_2(shard, axis, root):
    mine = lax.axis_index(axis) == root
    return lax.psum(jnp.where(mine, shard, jnp.zeros_like(shard)), axis)


def on_device_gather(
    amplitudes, slabs, couplings, occ_energy, vir_energy, occ_irrep, pair_i, pair_j, window_k, owner
):
    tile_blocks = slabs.shape[1]
    block_size = slabs.shape[3]
    block_area = block_size * block_size
    occ_count = occ_irrep.shape[0]
    local_pairs = amplitudes.shape[0]
    tile_index = lax.axis_index("vtile")
    gamma_irrep = lax.axis_index("irrep")
    beta_irreps = tile_index * tile_blocks + jnp.arange(tile_blocks, dtype=jnp.int32)
    pair_sym = jnp.bitwise_xor(occ_irrep[pair_i], occ_irrep[pair_j])
    send_index = jnp.bitwise_xor(beta_irreps[None, :], pair_sym[:, None])
    outgoing = jnp.take_along_axis(amplitudes, send_index[:, :, None], axis=1)
    local_slab = slabs[0, :, 0]
    gamma_energy = jnp.take(vir_energy, gamma_irrep, axis=0)
    beta_energy = vir_energy[beta_irreps]
    occ_keep = jnp.bitwise_xor(occ_irrep, gamma_irrep)

    def pair_term(amp_pair, occ_i, occ_j, hole_part, slab_data, k_irrep, k_energy):
        pair_irrep = jnp.bitwise_xor(occ_irrep[occ_i], occ_irrep[occ_j])
        alpha_irrep = jnp.bitwise_xor(
            jnp.bitwise_xor(pair_irrep, k_irrep), jnp.bitwise_xor(beta_irreps, gamma_irrep)
        )
        amp_sel = amp_pair[alpha_irrep].reshape(tile_blocks, block_size, block_size)
        particle = jnp.einsum(
            "mad,mdx->max", amp_sel, slab_data, preferred_element_type=jnp.float32
        )
        energy_a = vir_energy[alpha_irrep]
        base = occ_energy[occ_i] + occ_energy[occ_j] + k_energy
        denominator = (
            energy_a[:, :, None, None]
            + beta_energy[:, None, :, None]
            + gamma_energy[None, None, None, :]
            - base
        )
        triples = (
            (particle - hole_part) / denominator.reshape(tile_blocks, block_size, block_area)
        ).astype(jnp.bfloat16)
        contrib = jnp.einsum("max,mdx->mad", triples, slab_data, preferred_element_type=jnp.float32)
        return (
            jnp.zeros((8, block_area), jnp.float32)
            .at[alpha_irrep]
            .add(contrib.reshape(tile_blocks, block_area))
        )

    def coupling_rows(window, occ_j, k_irrep):
        y_column = jnp.take(couplings[window], occ_j, axis=1)
        keep_mask = jnp.bitwise_xor(occ_keep, jnp.bitwise_xor(occ_irrep[occ_j], k_irrep)) == 0
        return y_column.astype(jnp.float32) * keep_mask[:, None].astype(jnp.float32)

    empty_stash = jnp.zeros((local_pairs, occ_count, tile_blocks, block_area), jnp.bfloat16)
    empty_seen = jnp.zeros((local_pairs, occ_count), jnp.float32)
    stash = empty_stash
    seen = empty_seen
    piece_amp = lax.all_gather(outgoing, "pair", axis=0, tiled=True)
    piece_first = lax.all_gather(pair_i, "pair", axis=0, tiled=True)
    piece_second = lax.all_gather(pair_j, "pair", axis=0, tiled=True)
    match = piece_first[None, :] == pair_i[:, None]
    slot = jnp.where(match, piece_second[None, :], occ_count).astype(jnp.int32)
    row_index = jnp.broadcast_to(jnp.arange(local_pairs, dtype=jnp.int32)[:, None], slot.shape)
    spread = jnp.broadcast_to(piece_amp[None], (local_pairs,) + piece_amp.shape)
    stash = stash.at[row_index, slot].add(spread, mode="drop")
    seen = seen.at[row_index, slot].add(jnp.ones(slot.shape, jnp.float32), mode="drop")
    accumulated = jnp.zeros((local_pairs, 8, block_area), jnp.float32)
    for window in range(K_WIN):
        slab_data = spread_2(local_slab, "pair", owner[window])
        k_index = window_k[window]
        k_irrep = occ_irrep[k_index]
        k_energy = occ_energy[k_index]

        def folded_step(packed):
            amp_pair, occ_i, occ_j, slot_amp, slot_seen = packed
            coef_rows = coupling_rows(window, occ_j, k_irrep)
            coupling = (coef_rows * slot_seen[:, None]).astype(jnp.bfloat16)
            hole_part = jnp.einsum(
                "qmx,qc->mxc", slot_amp, coupling, preferred_element_type=jnp.float32
            )
            hole_part = hole_part.reshape(tile_blocks, block_size, block_area)
            return pair_term(amp_pair, occ_i, occ_j, hole_part, slab_data, k_irrep, k_energy)

        contrib_all = lax.map(folded_step, (amplitudes, pair_i, pair_j, stash, seen))
        accumulated = accumulated + contrib_all
    summed = lax.psum(accumulated, ("vtile", "irrep"))
    irrep_count = lax.axis_size("irrep")
    share = block_area // irrep_count
    summed = lax.dynamic_slice_in_dim(summed, tile_index * tile_blocks, tile_blocks, 1)
    return lax.dynamic_slice_in_dim(summed, gamma_irrep * share, share, 2)


GROUP = 16
LANE = 128
TILE = 256
STEP = 8


def tile_plan(rows):
    lanes = -(-GROUP * rows // TILE) * TILE
    depth = LANE // GROUP
    starts = []
    for first in range(0, lanes, TILE):
        lowest = min(first // rows, GROUP - depth)
        highest = min((first + TILE - 1) // rows, GROUP - 1)
        assert lowest >= 0 and highest < lowest + depth
        starts.append(lowest)
    return lanes, depth, starts


def b_chunks(block):
    unit = LANE // math.gcd(LANE, block)
    size = 2 * unit
    return [(first, min(size, block - first)) for first in range(0, block, size)]


def triples_kernel(last, *refs):
    eb_ref, vt_ref, v_ref, at_ref, arep_ref, ct_ref, mask_ref, ecol_ref, lrow_ref = refs[:9]
    o_ref, t_ref = refs[-2:]
    count, block = vt_ref.shape[1], vt_ref.shape[2]
    unroll = math.gcd(count, STEP)
    depth = mask_ref.shape[1] // GROUP
    tiles = mask_ref.shape[0]

    def some_b(step, carry):
        for tile in range(tiles):
            lanes = slice(tile * TILE, (tile + 1) * TILE)
            top = at_ref[0, :, lanes]
            for first in range(0, unroll, 2):
                results = []
                for b in (unroll * step + first, unroll * step + first + 1):
                    lhs = jnp.concatenate([vt_ref[0, b], ct_ref[0, 0, tile]], axis=1)
                    hole_amp = arep_ref[0, 0, b, :, lanes]
                    bottom = jnp.concatenate([hole_amp] * depth, axis=0) * mask_ref[tile]
                    rhs = jnp.concatenate([top, bottom], axis=0)
                    numer = jnp.dot(lhs, rhs, preferred_element_type=jnp.float32)
                    denom = (ecol_ref[...] + eb_ref[0, b]) + lrow_ref[0, 0, :, lanes]
                    results.append(numer / denom)
                start = pl.multiple_of((unroll * step + first) * block, 2 * block)
                t_ref[pl.ds(start, 2 * block), lanes] = jnp.concatenate(results, axis=0).astype(jnp.bfloat16)
        return carry

    lax.fori_loop(0, count // unroll, some_b, 0)

    def finish(tile, carry):
        lanes = pl.ds(pl.multiple_of(tile * TILE, TILE), TILE)
        contrib = jnp.dot(v_ref[0], t_ref[:, lanes], preferred_element_type=jnp.float32)
        if len(refs) == 12:
            contrib = contrib + refs[9][0, :, lanes]
        if last:
            o_ref[0, lanes, :] = contrib.T
        else:
            o_ref[0, :, lanes] = contrib
        return carry

    lax.fori_loop(0, tiles, finish, 0)


def triples_call(window, last, eb, vt, v, at, arep, ct, mask, ecol, lrow, total=None):
    _, count, block, _ = vt.shape
    groups, depth_rows, lanes = at.shape
    w = window
    tall, wide = pl.BlockSpec((1, lanes, block), lambda g: (g, 0, 0)), pl.BlockSpec((1, block, lanes), lambda g: (g, 0, 0))
    in_specs = [
        pl.BlockSpec(memory_space=pltpu.SMEM),
        pl.BlockSpec((1, count, block, LANE), lambda g: (w, 0, 0, 0)),
        pl.BlockSpec((1, block, count * block), lambda g: (w, 0, 0)),
        pl.BlockSpec((1, depth_rows, lanes), lambda g: (g, 0, 0)),
        pl.BlockSpec((1, 1, count, GROUP, lanes), lambda g: (w, g, 0, 0, 0)),
        pl.BlockSpec((1, 1) + ct.shape[2:], lambda g: (w, g, 0, 0, 0)),
        pl.BlockSpec(mask.shape, lambda g: (0, 0, 0)),
        pl.BlockSpec(ecol.shape, lambda g: (0, 0)),
        pl.BlockSpec((1, 1, 1, lanes), lambda g: (w, g, 0, 0)),
    ]
    operands = [eb[w : w + 1], vt, v, at, arep, ct, mask, ecol, lrow]
    if total is not None:
        in_specs.append(wide)
        operands.append(total)
    shape = (groups, lanes, block) if last else (groups, block, lanes)
    return pl.pallas_call(
        functools.partial(triples_kernel, last),
        grid=(groups,),
        in_specs=in_specs,
        out_specs=tall if last else wide,
        out_shape=jax.ShapeDtypeStruct(shape, jnp.float32),
        scratch_shapes=[pltpu.VMEM((count * block, lanes), jnp.bfloat16)],
        compiler_params=pltpu.CompilerParams(
            dimension_semantics=("arbitrary",), vmem_limit_bytes=40 * 1024 * 1024
        ),
        cost_estimate=pl.CostEstimate(
            flops=groups * count * block * lanes * 2 * (TILE + block) * 4,
            bytes_accessed=(arep.size + vt.size + v.size) * 2,
            transcendentals=groups * count * block * lanes,
        ),
        name="triples",
    )(*operands)


def swap_cores(x):
    return lax.ppermute(x, "irrep", [(0, 1), (1, 0)])


def across(x, bit):
    count = lax.axis_size("pair")
    return lax.ppermute(x, "pair", [(t, t ^ bit) for t in range(count)])


def pick(x, index):
    return lax.dynamic_index_in_dim(x, index, 0, keepdims=False)


def after(x, *others):
    return lax.optimization_barrier((x,) + others)[0]


class SlabPath:
    def __init__(self, owner, k_irrep, me, core):
        self.owner, self.k_irrep, self.core = owner, k_irrep, core
        self.windows = owner.shape[0]
        self.bits = [(me >> n) & 1 for n in range(4)]

    def from_here(self, bit):
        return ((self.owner >> bit) & 1) == self.bits[bit]

    def split_cores(self, slab):
        halves = slab.reshape((2, slab.shape[0] // 2) + slab.shape[1:])
        mine, theirs = pick(halves, self.core), swap_cores(pick(halves, 1 - self.core))
        same = self.bits[0] == self.core
        return jnp.where(same, mine, theirs), jnp.where(same, theirs, mine)

    def split_low(self, kept, came):
        def block(w, high, low):
            beta = (2 * high + low) ^ (self.k_irrep[w] & 3) ^ self.bits[0]
            return jnp.where(self.from_here(0)[w], pick(kept, beta), pick(came, beta))

        def blocks(low):
            return jnp.stack(
                [jnp.stack([block(w, high, low) for w in range(self.windows)]) for high in range(2)]
            )

        return blocks(self.bits[1]), blocks(1 - self.bits[1])

    def split_high(self, kept, came):
        here = self.from_here(1)[:, None, None]
        kept, leaving = [
            jnp.where(here, pick(kept, high), pick(came, high)) for high in (self.bits[2], 1 - self.bits[2])
        ]
        return kept, leaving

    def split_top(self, kept, came):
        blocks = jnp.where(self.from_here(2)[:, None, None], kept, came)
        mine, theirs = pick(blocks, self.core), swap_cores(pick(blocks, 1 - self.core))
        stays = (self.bits[3] ^ ((self.k_irrep[self.core] >> 2) & 1)) == self.core
        return jnp.where(stays, mine, theirs), jnp.where(stays, theirs, mine)

    def join(self, kept, came):
        block = jnp.where(self.from_here(3)[self.core], kept, came)
        other = swap_cores(block)
        first = self.core == 0
        return jnp.stack([jnp.where(first, block, other), jnp.where(first, other, block)])


def on_device_scatter(
    amplitudes, slabs, couplings, occ_energy, vir_energy, occ_irrep, pair_i, pair_j, window_k, owner
):
    betas, block = slabs.shape[1], slabs.shape[3]
    windows = window_k.shape[0]
    rows = block // lax.axis_size("irrep")
    share = rows * block
    chips = lax.axis_size("pair")
    local_pairs = pair_i.shape[0]
    pairs = chips * local_pairs
    groups = pairs // GROUP
    lanes, depth, starts = tile_plan(rows)
    me, core = lax.axis_index("pair"), lax.axis_index("irrep")
    gamma, m = me & 1, me >> 1
    k_irrep = occ_irrep[window_k]
    bf16 = jnp.bfloat16

    chunks = b_chunks(block)
    local = slabs[0, :, 0]
    path = SlabPath(owner, k_irrep, me, core)
    kept_x, sent_x = zip(
        *[path.split_cores(local[:, :, first * block : (first + size) * block]) for first, size in chunks]
    )
    x, leaving_x = [], []
    for leaving in sent_x:
        leaving_x.append(after(leaving, x[-1]) if x else leaving)
        x.append(across(leaving_x[-1], 1))
    kept_y, sent_y = [], []
    for kept, came in zip(kept_x, x):
        kept, leaving = path.split_low(kept, after(came, sent_y[-1]) if sent_y else came)
        kept_y.append(kept)
        sent_y.append(leaving)
    y = [across(leaving, 2) for leaving in sent_y]

    pair_sym = occ_irrep[pair_i] ^ occ_irrep[pair_j]
    mine = lax.dynamic_slice_in_dim(after(amplitudes, sent_x[0]), core * share, share, 2)
    target = jnp.arange(chips, dtype=jnp.int32)
    wanted = jnp.stack([target >> 1] + [(target >> 1) ^ (target & 1) ^ k_irrep[w] for w in range(windows)], 1)
    index = wanted[:, :, None] ^ pair_sym[None, None, :]
    kinds = 1 + windows
    labels = jnp.concatenate([pair_i, pair_j]).astype(bf16)
    labels = jnp.pad(labels, (0, share - labels.shape[0]))[None]
    stored = jnp.concatenate([mine.reshape(local_pairs * betas, share), labels], 0)
    index = index + betas * jnp.arange(local_pairs, dtype=jnp.int32)
    index = index.reshape(chips, kinds * local_pairs)
    index = jnp.pad(index, ((0, 0), (0, 1)), constant_values=local_pairs * betas).reshape(-1)
    chosen = (index[:, None] == jnp.arange(stored.shape[0], dtype=jnp.int32)[None, :]).astype(bf16)
    sent = jnp.einsum("rh,hx->rx", chosen, stored)
    sent = sent.reshape(chips, kinds * local_pairs + 1, share)
    came = lax.all_to_all(sent, "pair", 0, 0, tiled=True)
    came = after(came, sent_y[0], leaving_x[1])
    came = came.reshape(chips * (kinds * local_pairs + 1), share)
    label_rows = after(target, leaving_x[1]) * (kinds * local_pairs + 1) + kinds * local_pairs
    both = came[label_rows][:, : 2 * local_pairs].astype(jnp.int32).reshape(chips, 2, local_pairs)
    both = both.transpose(1, 0, 2).reshape(2, pairs)

    numbers = jnp.arange(pairs, dtype=jnp.int32)
    ahead = both[0][None, :] < both[0][:, None]
    tied = (both[0][None, :] == both[0][:, None]) & (numbers[None, :] < numbers[:, None])
    rank = jnp.sum((ahead | tied).astype(jnp.int32), axis=1)
    placed = (rank[None, :] == numbers[:, None]).astype(jnp.int32)
    order = jnp.sum(placed * numbers[None, :], axis=1)
    first = jnp.sum(placed * both[0][None, :], axis=1)
    second = jnp.sum(placed * both[1][None, :], axis=1)

    source = (order // local_pairs) * (kinds * local_pairs + 1) + order % local_pairs
    source = source[None, :] + local_pairs * jnp.arange(kinds, dtype=jnp.int32)[:, None]
    amps = came[source]
    amps = amps.reshape(kinds, groups, GROUP, rows, block)
    holes = amps[1:]
    used = GROUP * rows
    at = amps[0].transpose(0, 3, 1, 2).reshape(groups, block, used)
    at = jnp.pad(at, ((0, 0), (0, LANE - block), (0, lanes - used)))
    lane = jnp.arange(lanes, dtype=jnp.int32)
    spread = ((lane[None, :] % rows == jnp.arange(rows)[:, None]) & (lane < used)[None, :]).astype(bf16)
    lane_pair = lane // rows
    mask = jnp.stack([
        (jnp.repeat(start + jnp.arange(depth), GROUP)[:, None] == lane_pair[None, n * TILE : (n + 1) * TILE])
        for n, start in enumerate(starts)
    ]).astype(bf16)

    coupled = jnp.where(gamma == core, couplings, swap_cores(couplings))
    chosen = (second.reshape(groups, GROUP)[:, :, None] == jnp.arange(occ_irrep.shape[0])).astype(bf16)
    coupled = jnp.einsum("gql,wljc->wgqjc", chosen, coupled)
    coupled = jnp.einsum("gpj,wgqjc->wgcpq", chosen, coupled)
    sym_j = occ_irrep[second].reshape(groups, GROUP)
    keep = (sym_j[None, :, :, None] ^ sym_j[None, :, None, :] ^ gamma ^ k_irrep[:, None, None, None]) == 0
    coupled = -(coupled * keep[:, :, None].astype(bf16))
    ct = jnp.stack(
        [coupled[:, :, :, s : s + depth].reshape(windows, groups, block, depth * GROUP) for s in starts], 2
    )

    alpha = occ_irrep[first] ^ occ_irrep[second] ^ m
    energy_a = lax.dynamic_slice_in_dim(vir_energy, core * rows, rows, 1)[alpha]
    base = occ_energy[first] + occ_energy[second]
    lrow = energy_a[None] - (base[None] + occ_energy[window_k][:, None])[:, :, None]
    lrow = lrow.reshape(windows, groups, 1, used)
    lrow = jnp.pad(lrow, ((0, 0), (0, 0), (0, 0), (0, lanes - used)), constant_values=1.0)
    ecol = jnp.broadcast_to(pick(vir_energy, gamma)[:, None], (block, TILE))
    energy_b = vir_energy[m ^ gamma ^ k_irrep]

    eye = (jnp.arange(block)[:, None] == jnp.arange(LANE)[None, :]).astype(bf16)

    def spread_holes(chunk, *tokens):
        start, size = chunks[chunk]
        hole = after(holes[:, :, :, :, start : start + size], *tokens)
        return jnp.einsum("wgqab,ae->wgbqe", hole, spread)

    def run(chunk, w, v, total):
        start, size = chunks[chunk]
        vt = jnp.einsum("wdx,de->wxe", v, eye).reshape(windows, size, block, LANE)
        last = start + size == block and w == windows - 1
        energies = energy_b[:, start : start + size]
        return triples_call(w, last, energies, vt, v, at, areps[chunk], ct, mask, ecol, lrow, total)

    calls = [(chunk, w) for chunk in range(len(chunks)) for w in range(windows)]
    kept_z, sent_z, kept_h, sent_h, z, h, ready = {}, {}, {}, {}, {}, {}, {}

    def to_high(chunk, token=None):
        came_y = y[chunk] if token is None else after(y[chunk], token)
        kept_z[chunk], sent_z[chunk] = path.split_high(kept_y[chunk], came_y)
        z[chunk] = across(sent_z[chunk], 4)
        return sent_z[chunk]

    def to_top(chunk, token=None):
        came_z = z[chunk] if token is None else after(z[chunk], token)
        kept_h[chunk], sent_h[chunk] = path.split_top(kept_z[chunk], came_z)
        h[chunk] = across(sent_h[chunk], 8)
        return sent_h[chunk]

    def arrive(chunk, token=None):
        came_h = h[chunk] if token is None else after(h[chunk], token)
        ready[chunk] = path.join(kept_h[chunk], came_h)
        return ready[chunk]

    plan = {0: [(to_top, 1), (to_high, 2)], 1: [(arrive, 1), (to_top, 2)], 2: [(arrive, 2)]}
    to_high(0, amps)
    at = after(at, sent_z[0], sent_y[1], leaving_x[2])
    areps = [spread_holes(0, at)]
    to_top(0, areps[0])
    ct = after(ct, sent_h[0])
    arrive(0, ct)
    ready[0] = after(ready[0], to_high(1, sent_h[0]), sent_y[2])
    total = None
    for n, (chunk, w) in enumerate(calls):
        total = run(chunk, w, ready[chunk], total)
        issued = [move(number, total) for move, number in plan.get(n, [])]
        if n == 0:
            areps += [spread_holes(number, total) for number in range(1, len(chunks))]
        if issued:
            total = after(total, *issued)
    total = total[:, :used].reshape(pairs, share)[rank]
    cut = 8 if share % 8 == 0 else 1
    total = total.reshape(chips, local_pairs * cut, share // cut)
    came = lax.all_to_all(total, "pair", 0, 0, tiled=True)
    came = came.reshape(betas, 2, local_pairs, cut, share // cut)
    came = (came[:, 0] + came[:, 1]).reshape(betas, local_pairs, share)
    back = jnp.arange(betas, dtype=jnp.int32)[None, :] ^ pair_sym[:, None]
    return came[back, jnp.arange(local_pairs, dtype=jnp.int32)[:, None]]


def on_device(*args):
    betas, block = args[1].shape[1], args[1].shape[3]
    chips, cores = lax.axis_size("pair"), lax.axis_size("irrep")
    fits = lax.axis_size("vtile") == 1 and cores == 2 and betas == 8 and chips == betas * cores
    fits = fits and args[8].shape[0] == 2 and block % 2 == 0 and block < LANE
    if fits and args[5].shape[0] <= 256:
        return on_device_scatter(*args)
    return on_device_gather(*args)


def solution(mesh):
    placed = (
        P("pair", None, None),
        P("pair", "vtile", "irrep", None, None),
        P(None, None, None, "irrep"),
        P(),
        P(),
        P(),
        P("pair"),
        P("pair"),
        P(),
        P(),
    )
    return jax.shard_map(
        on_device,
        mesh=mesh,
        in_specs=placed,
        out_specs=P("pair", "vtile", "irrep"),
        check_vma=False,
    )
```

```python
import functools
import math

import jax
import jax.numpy as jnp
from jax import lax
from jax.experimental import pallas as pl
from jax.experimental.pallas import tpu as pltpu
from jax.sharding import PartitionSpec as P


K_WIN = 2


def spread_2(shard, axis, root):
    mine = lax.axis_index(axis) == root
    return lax.psum(jnp.where(mine, shard, jnp.zeros_like(shard)), axis)


def on_device_gather(
    amplitudes, slabs, couplings, occ_energy, vir_energy, occ_irrep, pair_i, pair_j, window_k, owner
):
    tile_blocks = slabs.shape[1]
    block_size = slabs.shape[3]
    block_area = block_size * block_size
    occ_count = occ_irrep.shape[0]
    local_pairs = amplitudes.shape[0]
    tile_index = lax.axis_index("vtile")
    gamma_irrep = lax.axis_index("irrep")
    beta_irreps = tile_index * tile_blocks + jnp.arange(tile_blocks, dtype=jnp.int32)
    pair_sym = jnp.bitwise_xor(occ_irrep[pair_i], occ_irrep[pair_j])
    send_index = jnp.bitwise_xor(beta_irreps[None, :], pair_sym[:, None])
    outgoing = jnp.take_along_axis(amplitudes, send_index[:, :, None], axis=1)
    local_slab = slabs[0, :, 0]
    gamma_energy = jnp.take(vir_energy, gamma_irrep, axis=0)
    beta_energy = vir_energy[beta_irreps]
    occ_keep = jnp.bitwise_xor(occ_irrep, gamma_irrep)

    def pair_term(amp_pair, occ_i, occ_j, hole_part, slab_data, k_irrep, k_energy):
        pair_irrep = jnp.bitwise_xor(occ_irrep[occ_i], occ_irrep[occ_j])
        alpha_irrep = jnp.bitwise_xor(
            jnp.bitwise_xor(pair_irrep, k_irrep), jnp.bitwise_xor(beta_irreps, gamma_irrep)
        )
        amp_sel = amp_pair[alpha_irrep].reshape(tile_blocks, block_size, block_size)
        particle = jnp.einsum(
            "mad,mdx->max", amp_sel, slab_data, preferred_element_type=jnp.float32
        )
        energy_a = vir_energy[alpha_irrep]
        base = occ_energy[occ_i] + occ_energy[occ_j] + k_energy
        denominator = (
            energy_a[:, :, None, None]
            + beta_energy[:, None, :, None]
            + gamma_energy[None, None, None, :]
            - base
        )
        triples = (
            (particle - hole_part) / denominator.reshape(tile_blocks, block_size, block_area)
        ).astype(jnp.bfloat16)
        contrib = jnp.einsum("max,mdx->mad", triples, slab_data, preferred_element_type=jnp.float32)
        return (
            jnp.zeros((8, block_area), jnp.float32)
            .at[alpha_irrep]
            .add(contrib.reshape(tile_blocks, block_area))
        )

    def coupling_rows(window, occ_j, k_irrep):
        y_column = jnp.take(couplings[window], occ_j, axis=1)
        keep_mask = jnp.bitwise_xor(occ_keep, jnp.bitwise_xor(occ_irrep[occ_j], k_irrep)) == 0
        return y_column.astype(jnp.float32) * keep_mask[:, None].astype(jnp.float32)

    empty_stash = jnp.zeros((local_pairs, occ_count, tile_blocks, block_area), jnp.bfloat16)
    empty_seen = jnp.zeros((local_pairs, occ_count), jnp.float32)
    stash = empty_stash
    seen = empty_seen
    piece_amp = lax.all_gather(outgoing, "pair", axis=0, tiled=True)
    piece_first = lax.all_gather(pair_i, "pair", axis=0, tiled=True)
    piece_second = lax.all_gather(pair_j, "pair", axis=0, tiled=True)
    match = piece_first[None, :] == pair_i[:, None]
    slot = jnp.where(match, piece_second[None, :], occ_count).astype(jnp.int32)
    row_index = jnp.broadcast_to(jnp.arange(local_pairs, dtype=jnp.int32)[:, None], slot.shape)
    spread = jnp.broadcast_to(piece_amp[None], (local_pairs,) + piece_amp.shape)
    stash = stash.at[row_index, slot].add(spread, mode="drop")
    seen = seen.at[row_index, slot].add(jnp.ones(slot.shape, jnp.float32), mode="drop")
    accumulated = jnp.zeros((local_pairs, 8, block_area), jnp.float32)
    for window in range(K_WIN):
        slab_data = spread_2(local_slab, "pair", owner[window])
        k_index = window_k[window]
        k_irrep = occ_irrep[k_index]
        k_energy = occ_energy[k_index]

        def folded_step(packed):
            amp_pair, occ_i, occ_j, slot_amp, slot_seen = packed
            coef_rows = coupling_rows(window, occ_j, k_irrep)
            coupling = (coef_rows * slot_seen[:, None]).astype(jnp.bfloat16)
            hole_part = jnp.einsum(
                "qmx,qc->mxc", slot_amp, coupling, preferred_element_type=jnp.float32
            )
            hole_part = hole_part.reshape(tile_blocks, block_size, block_area)
            return pair_term(amp_pair, occ_i, occ_j, hole_part, slab_data, k_irrep, k_energy)

        contrib_all = lax.map(folded_step, (amplitudes, pair_i, pair_j, stash, seen))
        accumulated = accumulated + contrib_all
    summed = lax.psum(accumulated, ("vtile", "irrep"))
    irrep_count = lax.axis_size("irrep")
    share = block_area // irrep_count
    summed = lax.dynamic_slice_in_dim(summed, tile_index * tile_blocks, tile_blocks, 1)
    return lax.dynamic_slice_in_dim(summed, gamma_irrep * share, share, 2)


GROUP = 16
LANE = 128
TILE = 256
STEP = 8


def tile_plan(rows):
    lanes = -(-GROUP * rows // TILE) * TILE
    depth = LANE // GROUP
    starts = []
    for first in range(0, lanes, TILE):
        lowest = min(first // rows, GROUP - depth)
        highest = min((first + TILE - 1) // rows, GROUP - 1)
        assert lowest >= 0 and highest < lowest + depth
        starts.append(lowest)
    return lanes, depth, starts


def b_chunks(block):
    unit = LANE // math.gcd(LANE, block)
    sizes = (unit, unit, 2 * unit, block - 4 * unit)
    return [(sum(sizes[:n]), size) for n, size in enumerate(sizes)]


def triples_kernel(last, *refs):
    eb_ref, vt_ref, v_ref, at_ref, arep_ref, ct_ref, mask_ref, ecol_ref, lrow_ref = refs[:9]
    o_ref, t_ref = refs[-2:]
    count, block = vt_ref.shape[1], vt_ref.shape[2]
    unroll = math.gcd(count, STEP)
    depth = mask_ref.shape[1] // GROUP
    tiles = mask_ref.shape[0]

    def some_b(step, carry):
        for tile in range(tiles):
            lanes = slice(tile * TILE, (tile + 1) * TILE)
            top = at_ref[0, :, lanes]
            for first in range(0, unroll, 2):
                results = []
                for b in (unroll * step + first, unroll * step + first + 1):
                    lhs = jnp.concatenate([vt_ref[0, b], ct_ref[0, 0, tile]], axis=1)
                    hole_amp = arep_ref[0, 0, b, :, lanes]
                    bottom = jnp.concatenate([hole_amp] * depth, axis=0) * mask_ref[tile]
                    rhs = jnp.concatenate([top, bottom], axis=0)
                    numer = jnp.dot(lhs, rhs, preferred_element_type=jnp.float32)
                    denom = (ecol_ref[...] + eb_ref[0, b]) + lrow_ref[0, 0, :, lanes]
                    results.append(numer / denom)
                start = pl.multiple_of((unroll * step + first) * block, 2 * block)
                t_ref[pl.ds(start, 2 * block), lanes] = jnp.concatenate(results, axis=0).astype(jnp.bfloat16)
        return carry

    lax.fori_loop(0, count // unroll, some_b, 0)

    def finish(tile, carry):
        lanes = pl.ds(pl.multiple_of(tile * TILE, TILE), TILE)
        contrib = jnp.dot(v_ref[0], t_ref[:, lanes], preferred_element_type=jnp.float32)
        if len(refs) == 12:
            contrib = contrib + refs[9][0, :, lanes]
        if last:
            o_ref[0, lanes, :] = contrib.T
        else:
            o_ref[0, :, lanes] = contrib
        return carry

    lax.fori_loop(0, tiles, finish, 0)


def triples_call(window, last, eb, vt, v, at, arep, ct, mask, ecol, lrow, total=None):
    _, count, block, _ = vt.shape
    groups, depth_rows, lanes = at.shape
    w = window
    tall, wide = pl.BlockSpec((1, lanes, block), lambda g: (g, 0, 0)), pl.BlockSpec((1, block, lanes), lambda g: (g, 0, 0))
    in_specs = [
        pl.BlockSpec(memory_space=pltpu.SMEM),
        pl.BlockSpec((1, count, block, LANE), lambda g: (w, 0, 0, 0)),
        pl.BlockSpec((1, block, count * block), lambda g: (w, 0, 0)),
        pl.BlockSpec((1, depth_rows, lanes), lambda g: (g, 0, 0)),
        pl.BlockSpec((1, 1, count, GROUP, lanes), lambda g: (w, g, 0, 0, 0)),
        pl.BlockSpec((1, 1) + ct.shape[2:], lambda g: (w, g, 0, 0, 0)),
        pl.BlockSpec(mask.shape, lambda g: (0, 0, 0)),
        pl.BlockSpec(ecol.shape, lambda g: (0, 0)),
        pl.BlockSpec((1, 1, 1, lanes), lambda g: (w, g, 0, 0)),
    ]
    operands = [eb[w : w + 1], vt, v, at, arep, ct, mask, ecol, lrow]
    if total is not None:
        in_specs.append(wide)
        operands.append(total)
    shape = (groups, lanes, block) if last else (groups, block, lanes)
    return pl.pallas_call(
        functools.partial(triples_kernel, last),
        grid=(groups,),
        in_specs=in_specs,
        out_specs=tall if last else wide,
        out_shape=jax.ShapeDtypeStruct(shape, jnp.float32),
        scratch_shapes=[pltpu.VMEM((count * block, lanes), jnp.bfloat16)],
        compiler_params=pltpu.CompilerParams(
            dimension_semantics=("arbitrary",), vmem_limit_bytes=40 * 1024 * 1024
        ),
        cost_estimate=pl.CostEstimate(
            flops=groups * count * block * lanes * 2 * (TILE + block) * 4,
            bytes_accessed=(arep.size + vt.size + v.size) * 2,
            transcendentals=groups * count * block * lanes,
        ),
        name="triples",
    )(*operands)


def swap_cores(x):
    return lax.ppermute(x, "irrep", [(0, 1), (1, 0)])


def across(x, bit):
    count = lax.axis_size("pair")
    return lax.ppermute(x, "pair", [(t, t ^ bit) for t in range(count)])


def pick(x, index):
    return lax.dynamic_index_in_dim(x, index, 0, keepdims=False)


def after(x, *others):
    return lax.optimization_barrier((x,) + others)[0]


class SlabPath:
    def __init__(self, owner, k_irrep, me, core):
        self.owner, self.k_irrep, self.core = owner, k_irrep, core
        self.windows = owner.shape[0]
        self.bits = [(me >> n) & 1 for n in range(4)]

    def from_here(self, bit):
        return ((self.owner >> bit) & 1) == self.bits[bit]

    def split_cores(self, slab):
        halves = slab.reshape((2, slab.shape[0] // 2) + slab.shape[1:])
        mine, theirs = pick(halves, self.core), swap_cores(pick(halves, 1 - self.core))
        same = self.bits[0] == self.core
        return jnp.where(same, mine, theirs), jnp.where(same, theirs, mine)

    def split_low(self, kept, came):
        def block(w, high, low):
            beta = (2 * high + low) ^ (self.k_irrep[w] & 3) ^ self.bits[0]
            return jnp.where(self.from_here(0)[w], pick(kept, beta), pick(came, beta))

        def blocks(low):
            return jnp.stack(
                [jnp.stack([block(w, high, low) for w in range(self.windows)]) for high in range(2)]
            )

        return blocks(self.bits[1]), blocks(1 - self.bits[1])

    def split_high(self, kept, came):
        here = self.from_here(1)[:, None, None]
        kept, leaving = [
            jnp.where(here, pick(kept, high), pick(came, high)) for high in (self.bits[2], 1 - self.bits[2])
        ]
        return kept, leaving

    def split_top(self, kept, came):
        blocks = jnp.where(self.from_here(2)[:, None, None], kept, came)
        mine, theirs = pick(blocks, self.core), swap_cores(pick(blocks, 1 - self.core))
        stays = (self.bits[3] ^ ((self.k_irrep[self.core] >> 2) & 1)) == self.core
        return jnp.where(stays, mine, theirs), jnp.where(stays, theirs, mine)

    def join(self, kept, came):
        block = jnp.where(self.from_here(3)[self.core], kept, came)
        other = swap_cores(block)
        first = self.core == 0
        return jnp.stack([jnp.where(first, block, other), jnp.where(first, other, block)])


def on_device_scatter(
    amplitudes, slabs, couplings, occ_energy, vir_energy, occ_irrep, pair_i, pair_j, window_k, owner
):
    betas, block = slabs.shape[1], slabs.shape[3]
    windows = window_k.shape[0]
    rows = block // lax.axis_size("irrep")
    share = rows * block
    chips = lax.axis_size("pair")
    local_pairs = pair_i.shape[0]
    pairs = chips * local_pairs
    groups = pairs // GROUP
    lanes, depth, starts = tile_plan(rows)
    me, core = lax.axis_index("pair"), lax.axis_index("irrep")
    gamma, m = me & 1, me >> 1
    k_irrep = occ_irrep[window_k]
    bf16 = jnp.bfloat16

    chunks = b_chunks(block)
    local = slabs[0, :, 0]
    path = SlabPath(owner, k_irrep, me, core)
    kept_x, sent_x = zip(
        *[path.split_cores(local[:, :, first * block : (first + size) * block]) for first, size in chunks]
    )
    x, leaving_x = [], []
    for leaving in sent_x:
        leaving_x.append(after(leaving, x[-1]) if x else leaving)
        x.append(across(leaving_x[-1], 1))
    kept_y, sent_y, kept_z, sent_z, kept_h, sent_h = {}, {}, {}, {}, {}, {}
    y, z, h, ready = {}, {}, {}, {}

    def to_low(chunk, *tokens):
        kept_y[chunk], sent_y[chunk] = path.split_low(kept_x[chunk], after(x[chunk], *tokens))
        y[chunk] = across(sent_y[chunk], 2)

    def to_high(chunk, *tokens):
        kept_z[chunk], sent_z[chunk] = path.split_high(kept_y[chunk], after(y[chunk], *tokens))
        z[chunk] = across(sent_z[chunk], 4)

    def to_top(chunk, *tokens):
        kept_h[chunk], sent_h[chunk] = path.split_top(kept_z[chunk], after(z[chunk], *tokens))
        h[chunk] = across(sent_h[chunk], 8)

    def arrive(chunk, *tokens):
        ready[chunk] = path.join(kept_h[chunk], after(h[chunk], *tokens))

    to_low(0, sent_x[0])
    to_low(1, sent_y[0])
    to_high(0, sent_y[1])

    pair_sym = occ_irrep[pair_i] ^ occ_irrep[pair_j]
    mine = lax.dynamic_slice_in_dim(after(amplitudes, sent_x[0]), core * share, share, 2)
    target = jnp.arange(chips, dtype=jnp.int32)
    wanted = jnp.stack([target >> 1] + [(target >> 1) ^ (target & 1) ^ k_irrep[w] for w in range(windows)], 1)
    index = wanted[:, :, None] ^ pair_sym[None, None, :]
    kinds = 1 + windows
    labels = jnp.concatenate([pair_i, pair_j]).astype(bf16)
    labels = jnp.pad(labels, (0, share - labels.shape[0]))[None]
    stored = jnp.concatenate([mine.reshape(local_pairs * betas, share), labels], 0)
    index = index + betas * jnp.arange(local_pairs, dtype=jnp.int32)
    index = index.reshape(chips, kinds * local_pairs)
    index = jnp.pad(index, ((0, 0), (0, 1)), constant_values=local_pairs * betas).reshape(-1)
    chosen = (index[:, None] == jnp.arange(stored.shape[0], dtype=jnp.int32)[None, :]).astype(bf16)
    sent = jnp.einsum("rh,hx->rx", chosen, stored)
    sent = sent.reshape(chips, kinds * local_pairs + 1, share)
    came = lax.all_to_all(sent, "pair", 0, 0, tiled=True)
    came = after(came, sent_z[0], leaving_x[2])
    came = came.reshape(chips * (kinds * local_pairs + 1), share)
    label_rows = after(target, leaving_x[1]) * (kinds * local_pairs + 1) + kinds * local_pairs
    both = came[label_rows][:, : 2 * local_pairs].astype(jnp.int32).reshape(chips, 2, local_pairs)
    both = both.transpose(1, 0, 2).reshape(2, pairs)

    numbers = jnp.arange(pairs, dtype=jnp.int32)
    ahead = both[0][None, :] < both[0][:, None]
    tied = (both[0][None, :] == both[0][:, None]) & (numbers[None, :] < numbers[:, None])
    rank = jnp.sum((ahead | tied).astype(jnp.int32), axis=1)
    placed = (rank[None, :] == numbers[:, None]).astype(jnp.int32)
    order = jnp.sum(placed * numbers[None, :], axis=1)
    first = jnp.sum(placed * both[0][None, :], axis=1)
    second = jnp.sum(placed * both[1][None, :], axis=1)

    source = (order // local_pairs) * (kinds * local_pairs + 1) + order % local_pairs
    source = source[None, :] + local_pairs * jnp.arange(kinds, dtype=jnp.int32)[:, None]
    amps = came[source]
    amps = amps.reshape(kinds, groups, GROUP, rows, block)
    holes = amps[1:]
    used = GROUP * rows
    at = amps[0].transpose(0, 3, 1, 2).reshape(groups, block, used)
    at = jnp.pad(at, ((0, 0), (0, LANE - block), (0, lanes - used)))
    lane = jnp.arange(lanes, dtype=jnp.int32)
    spread = ((lane[None, :] % rows == jnp.arange(rows)[:, None]) & (lane < used)[None, :]).astype(bf16)
    lane_pair = lane // rows
    mask = jnp.stack([
        (jnp.repeat(start + jnp.arange(depth), GROUP)[:, None] == lane_pair[None, n * TILE : (n + 1) * TILE])
        for n, start in enumerate(starts)
    ]).astype(bf16)

    coupled = jnp.where(gamma == core, couplings, swap_cores(couplings))
    chosen = (second.reshape(groups, GROUP)[:, :, None] == jnp.arange(occ_irrep.shape[0])).astype(bf16)
    coupled = jnp.einsum("gql,wljc->wgqjc", chosen, coupled)
    coupled = jnp.einsum("gpj,wgqjc->wgcpq", chosen, coupled)
    sym_j = occ_irrep[second].reshape(groups, GROUP)
    keep = (sym_j[None, :, :, None] ^ sym_j[None, :, None, :] ^ gamma ^ k_irrep[:, None, None, None]) == 0
    coupled = -(coupled * keep[:, :, None].astype(bf16))
    ct = jnp.stack(
        [coupled[:, :, :, s : s + depth].reshape(windows, groups, block, depth * GROUP) for s in starts], 2
    )

    alpha = occ_irrep[first] ^ occ_irrep[second] ^ m
    energy_a = lax.dynamic_slice_in_dim(vir_energy, core * rows, rows, 1)[alpha]
    base = occ_energy[first] + occ_energy[second]
    lrow = energy_a[None] - (base[None] + occ_energy[window_k][:, None])[:, :, None]
    lrow = lrow.reshape(windows, groups, 1, used)
    lrow = jnp.pad(lrow, ((0, 0), (0, 0), (0, 0), (0, lanes - used)), constant_values=1.0)
    ecol = jnp.broadcast_to(pick(vir_energy, gamma)[:, None], (block, TILE))
    energy_b = vir_energy[m ^ gamma ^ k_irrep]

    eye = (jnp.arange(block)[:, None] == jnp.arange(LANE)[None, :]).astype(bf16)

    def spread_holes(chunk, *tokens):
        start, size = chunks[chunk]
        hole = after(holes[:, :, :, :, start : start + size], *tokens)
        return jnp.einsum("wgqab,ae->wgbqe", hole, spread)

    def run(chunk, w, v, total):
        start, size = chunks[chunk]
        vt = jnp.einsum("wdx,de->wxe", v, eye).reshape(windows, size, block, LANE)
        last = start + size == block and w == windows - 1
        energies = energy_b[:, start : start + size]
        return triples_call(w, last, energies, vt, v, at, areps[chunk], ct, mask, ecol, lrow, total)

    calls = [(chunk, w) for chunk in range(len(chunks)) for w in range(windows)]
    to_top(0, amps)
    to_high(1, sent_h[0])
    to_low(2, sent_z[1])
    at = after(at, sent_y[2], leaving_x[3])
    areps = {0: spread_holes(0, at)}
    ct = after(ct, areps[0])
    arrive(0, ct)
    to_top(1, ready[0])
    ready[0] = after(ready[0], sent_h[1])
    total = None
    for n, (chunk, w) in enumerate(calls):
        total = run(chunk, w, ready[chunk], total)
        if n == 0:
            arrive(1, total)
            areps[1] = spread_holes(1, total)
            total = after(total, ready[1])
        elif n == 1:
            to_low(3, total)
            total = after(total, sent_y[3])
        elif n == 2:
            to_high(2, total)
            total = after(total, sent_z[2])
        elif n == 3:
            areps[2] = spread_holes(2, total)
            to_top(2, areps[2])
            areps[3] = spread_holes(3, sent_h[2])
            to_high(3, areps[3])
            arrive(2, sent_z[3])
            to_top(3, ready[2])
            total = after(total, sent_h[3])
        elif n == 4:
            arrive(3, total)
            total = after(total, ready[3])
    total = total[:, :used].reshape(pairs, share)[rank]
    cut = 8 if share % 8 == 0 else 1
    total = total.reshape(chips, local_pairs * cut, share // cut)
    came = lax.all_to_all(total, "pair", 0, 0, tiled=True)
    came = came.reshape(betas, 2, local_pairs, cut, share // cut)
    came = (came[:, 0] + came[:, 1]).reshape(betas, local_pairs, share)
    back = jnp.arange(betas, dtype=jnp.int32)[None, :] ^ pair_sym[:, None]
    return came[back, jnp.arange(local_pairs, dtype=jnp.int32)[:, None]]


def on_device(*args):
    betas, block = args[1].shape[1], args[1].shape[3]
    chips, cores = lax.axis_size("pair"), lax.axis_size("irrep")
    fits = lax.axis_size("vtile") == 1 and cores == 2 and betas == 8 and chips == betas * cores
    fits = fits and args[8].shape[0] == 2 and block % 2 == 0 and block < LANE
    fits = fits and all(size > 0 and size % 2 == 0 for _, size in b_chunks(block))
    if fits and args[5].shape[0] <= 256:
        return on_device_scatter(*args)
    return on_device_gather(*args)


def solution(mesh):
    placed = (
        P("pair", None, None),
        P("pair", "vtile", "irrep", None, None),
        P(None, None, None, "irrep"),
        P(),
        P(),
        P(),
        P("pair"),
        P("pair"),
        P(),
        P(),
    )
    return jax.shard_map(
        on_device,
        mesh=mesh,
        in_specs=placed,
        out_specs=P("pair", "vtile", "irrep"),
        check_vma=False,
    )
```

```python
import functools
import math

import jax
import jax.numpy as jnp
from jax import lax
from jax.experimental import pallas as pl
from jax.experimental.pallas import tpu as pltpu
from jax.sharding import PartitionSpec as P


K_WIN = 2


def spread_2(shard, axis, root):
    mine = lax.axis_index(axis) == root
    return lax.psum(jnp.where(mine, shard, jnp.zeros_like(shard)), axis)


def on_device_gather(
    amplitudes, slabs, couplings, occ_energy, vir_energy, occ_irrep, pair_i, pair_j, window_k, owner
):
    tile_blocks = slabs.shape[1]
    block_size = slabs.shape[3]
    block_area = block_size * block_size
    occ_count = occ_irrep.shape[0]
    local_pairs = amplitudes.shape[0]
    tile_index = lax.axis_index("vtile")
    gamma_irrep = lax.axis_index("irrep")
    beta_irreps = tile_index * tile_blocks + jnp.arange(tile_blocks, dtype=jnp.int32)
    pair_sym = jnp.bitwise_xor(occ_irrep[pair_i], occ_irrep[pair_j])
    send_index = jnp.bitwise_xor(beta_irreps[None, :], pair_sym[:, None])
    outgoing = jnp.take_along_axis(amplitudes, send_index[:, :, None], axis=1)
    local_slab = slabs[0, :, 0]
    gamma_energy = jnp.take(vir_energy, gamma_irrep, axis=0)
    beta_energy = vir_energy[beta_irreps]
    occ_keep = jnp.bitwise_xor(occ_irrep, gamma_irrep)

    def pair_term(amp_pair, occ_i, occ_j, hole_part, slab_data, k_irrep, k_energy):
        pair_irrep = jnp.bitwise_xor(occ_irrep[occ_i], occ_irrep[occ_j])
        alpha_irrep = jnp.bitwise_xor(
            jnp.bitwise_xor(pair_irrep, k_irrep), jnp.bitwise_xor(beta_irreps, gamma_irrep)
        )
        amp_sel = amp_pair[alpha_irrep].reshape(tile_blocks, block_size, block_size)
        particle = jnp.einsum(
            "mad,mdx->max", amp_sel, slab_data, preferred_element_type=jnp.float32
        )
        energy_a = vir_energy[alpha_irrep]
        base = occ_energy[occ_i] + occ_energy[occ_j] + k_energy
        denominator = (
            energy_a[:, :, None, None]
            + beta_energy[:, None, :, None]
            + gamma_energy[None, None, None, :]
            - base
        )
        triples = (
            (particle - hole_part) / denominator.reshape(tile_blocks, block_size, block_area)
        ).astype(jnp.bfloat16)
        contrib = jnp.einsum("max,mdx->mad", triples, slab_data, preferred_element_type=jnp.float32)
        return (
            jnp.zeros((8, block_area), jnp.float32)
            .at[alpha_irrep]
            .add(contrib.reshape(tile_blocks, block_area))
        )

    def coupling_rows(window, occ_j, k_irrep):
        y_column = jnp.take(couplings[window], occ_j, axis=1)
        keep_mask = jnp.bitwise_xor(occ_keep, jnp.bitwise_xor(occ_irrep[occ_j], k_irrep)) == 0
        return y_column.astype(jnp.float32) * keep_mask[:, None].astype(jnp.float32)

    empty_stash = jnp.zeros((local_pairs, occ_count, tile_blocks, block_area), jnp.bfloat16)
    empty_seen = jnp.zeros((local_pairs, occ_count), jnp.float32)
    stash = empty_stash
    seen = empty_seen
    piece_amp = lax.all_gather(outgoing, "pair", axis=0, tiled=True)
    piece_first = lax.all_gather(pair_i, "pair", axis=0, tiled=True)
    piece_second = lax.all_gather(pair_j, "pair", axis=0, tiled=True)
    match = piece_first[None, :] == pair_i[:, None]
    slot = jnp.where(match, piece_second[None, :], occ_count).astype(jnp.int32)
    row_index = jnp.broadcast_to(jnp.arange(local_pairs, dtype=jnp.int32)[:, None], slot.shape)
    spread = jnp.broadcast_to(piece_amp[None], (local_pairs,) + piece_amp.shape)
    stash = stash.at[row_index, slot].add(spread, mode="drop")
    seen = seen.at[row_index, slot].add(jnp.ones(slot.shape, jnp.float32), mode="drop")
    accumulated = jnp.zeros((local_pairs, 8, block_area), jnp.float32)
    for window in range(K_WIN):
        slab_data = spread_2(local_slab, "pair", owner[window])
        k_index = window_k[window]
        k_irrep = occ_irrep[k_index]
        k_energy = occ_energy[k_index]

        def folded_step(packed):
            amp_pair, occ_i, occ_j, slot_amp, slot_seen = packed
            coef_rows = coupling_rows(window, occ_j, k_irrep)
            coupling = (coef_rows * slot_seen[:, None]).astype(jnp.bfloat16)
            hole_part = jnp.einsum(
                "qmx,qc->mxc", slot_amp, coupling, preferred_element_type=jnp.float32
            )
            hole_part = hole_part.reshape(tile_blocks, block_size, block_area)
            return pair_term(amp_pair, occ_i, occ_j, hole_part, slab_data, k_irrep, k_energy)

        contrib_all = lax.map(folded_step, (amplitudes, pair_i, pair_j, stash, seen))
        accumulated = accumulated + contrib_all
    summed = lax.psum(accumulated, ("vtile", "irrep"))
    irrep_count = lax.axis_size("irrep")
    share = block_area // irrep_count
    summed = lax.dynamic_slice_in_dim(summed, tile_index * tile_blocks, tile_blocks, 1)
    return lax.dynamic_slice_in_dim(summed, gamma_irrep * share, share, 2)


GROUP = 16
LANE = 128
TILE = 256
STEP = 8


def tile_plan(rows):
    lanes = -(-GROUP * rows // TILE) * TILE
    depth = LANE // GROUP
    starts = []
    for first in range(0, lanes, TILE):
        lowest = min(first // rows, GROUP - depth)
        highest = min((first + TILE - 1) // rows, GROUP - 1)
        assert lowest >= 0 and highest < lowest + depth
        starts.append(lowest)
    return lanes, depth, starts


def b_chunks(block):
    unit = LANE // math.gcd(LANE, block)
    sizes = (unit, unit, 2 * unit, block - 4 * unit)
    return [(sum(sizes[:n]), size) for n, size in enumerate(sizes)]


def triples_kernel(last, *refs):
    eb_ref, vt_ref, v_ref, at_ref, arep_ref, ct_ref, mask_ref, ecol_ref, lrow_ref = refs[:9]
    o_ref, t_ref = refs[-2:]
    count, block = vt_ref.shape[1], vt_ref.shape[2]
    unroll = math.gcd(count, STEP)
    depth = mask_ref.shape[1] // GROUP
    tiles = mask_ref.shape[0]

    def some_b(step, carry):
        for tile in range(tiles):
            lanes = slice(tile * TILE, (tile + 1) * TILE)
            top = at_ref[0, :, lanes]
            for first in range(0, unroll, 2):
                results = []
                for b in (unroll * step + first, unroll * step + first + 1):
                    lhs = jnp.concatenate([vt_ref[0, b], ct_ref[0, 0, tile]], axis=1)
                    hole_amp = arep_ref[0, 0, b, :, lanes]
                    bottom = jnp.concatenate([hole_amp] * depth, axis=0) * mask_ref[tile]
                    rhs = jnp.concatenate([top, bottom], axis=0)
                    numer = jnp.dot(lhs, rhs, preferred_element_type=jnp.float32)
                    denom = (ecol_ref[...] + eb_ref[0, b]) + lrow_ref[0, 0, :, lanes]
                    results.append(numer / denom)
                start = pl.multiple_of((unroll * step + first) * block, 2 * block)
                t_ref[pl.ds(start, 2 * block), lanes] = jnp.concatenate(results, axis=0).astype(jnp.bfloat16)
        return carry

    lax.fori_loop(0, count // unroll, some_b, 0)

    def finish(tile, carry):
        lanes = pl.ds(pl.multiple_of(tile * TILE, TILE), TILE)
        contrib = jnp.dot(v_ref[0], t_ref[:, lanes], preferred_element_type=jnp.float32)
        if len(refs) == 12:
            contrib = contrib + refs[9][0, :, lanes]
        if last:
            o_ref[0, lanes, :] = contrib.T
        else:
            o_ref[0, :, lanes] = contrib
        return carry

    lax.fori_loop(0, tiles, finish, 0)


def triples_call(window, last, eb, vt, v, at, arep, ct, mask, ecol, lrow, total=None):
    _, count, block, _ = vt.shape
    groups, depth_rows, lanes = at.shape
    w = window
    tall, wide = pl.BlockSpec((1, lanes, block), lambda g: (g, 0, 0)), pl.BlockSpec((1, block, lanes), lambda g: (g, 0, 0))
    in_specs = [
        pl.BlockSpec(memory_space=pltpu.SMEM),
        pl.BlockSpec((1, count, block, LANE), lambda g: (w, 0, 0, 0)),
        pl.BlockSpec((1, block, count * block), lambda g: (w, 0, 0)),
        pl.BlockSpec((1, depth_rows, lanes), lambda g: (g, 0, 0)),
        pl.BlockSpec((1, 1, count, GROUP, lanes), lambda g: (w, g, 0, 0, 0)),
        pl.BlockSpec((1, 1) + ct.shape[2:], lambda g: (w, g, 0, 0, 0)),
        pl.BlockSpec(mask.shape, lambda g: (0, 0, 0)),
        pl.BlockSpec(ecol.shape, lambda g: (0, 0)),
        pl.BlockSpec((1, 1, 1, lanes), lambda g: (w, g, 0, 0)),
    ]
    operands = [eb[w : w + 1], vt, v, at, arep, ct, mask, ecol, lrow]
    if total is not None:
        in_specs.append(wide)
        operands.append(total)
    shape = (groups, lanes, block) if last else (groups, block, lanes)
    return pl.pallas_call(
        functools.partial(triples_kernel, last),
        grid=(groups,),
        in_specs=in_specs,
        out_specs=tall if last else wide,
        out_shape=jax.ShapeDtypeStruct(shape, jnp.float32),
        scratch_shapes=[pltpu.VMEM((count * block, lanes), jnp.bfloat16)],
        compiler_params=pltpu.CompilerParams(
            dimension_semantics=("arbitrary",), vmem_limit_bytes=40 * 1024 * 1024
        ),
        cost_estimate=pl.CostEstimate(
            flops=groups * count * block * lanes * 2 * (TILE + block) * 4,
            bytes_accessed=(arep.size + vt.size + v.size) * 2,
            transcendentals=groups * count * block * lanes,
        ),
        name="triples",
    )(*operands)


def swap_cores(x):
    return lax.ppermute(x, "irrep", [(0, 1), (1, 0)])


def across(x, bit):
    count = lax.axis_size("pair")
    return lax.ppermute(x, "pair", [(t, t ^ bit) for t in range(count)])


def pick(x, index):
    return lax.dynamic_index_in_dim(x, index, 0, keepdims=False)


def after(x, *others):
    return lax.optimization_barrier((x,) + others)[0]


class SlabPath:
    def __init__(self, owner, k_irrep, me, core):
        self.owner, self.k_irrep, self.core = owner, k_irrep, core
        self.windows = owner.shape[0]
        self.bits = [(me >> n) & 1 for n in range(4)]

    def from_here(self, bit):
        return ((self.owner >> bit) & 1) == self.bits[bit]

    def split_cores(self, slab):
        halves = slab.reshape((2, slab.shape[0] // 2) + slab.shape[1:])
        mine, theirs = pick(halves, self.core), swap_cores(pick(halves, 1 - self.core))
        same = self.bits[0] == self.core
        return jnp.where(same, mine, theirs), jnp.where(same, theirs, mine)

    def split_low(self, kept, came):
        def block(w, high, low):
            beta = (2 * high + low) ^ (self.k_irrep[w] & 3) ^ self.bits[0]
            return jnp.where(self.from_here(0)[w], pick(kept, beta), pick(came, beta))

        def blocks(low):
            return jnp.stack(
                [jnp.stack([block(w, high, low) for w in range(self.windows)]) for high in range(2)]
            )

        return blocks(self.bits[1]), blocks(1 - self.bits[1])

    def split_high(self, kept, came):
        here = self.from_here(1)[:, None, None]
        kept, leaving = [
            jnp.where(here, pick(kept, high), pick(came, high)) for high in (self.bits[2], 1 - self.bits[2])
        ]
        return kept, leaving

    def split_top(self, kept, came):
        blocks = jnp.where(self.from_here(2)[:, None, None], kept, came)
        mine, theirs = pick(blocks, self.core), swap_cores(pick(blocks, 1 - self.core))
        stays = (self.bits[3] ^ ((self.k_irrep[self.core] >> 2) & 1)) == self.core
        return jnp.where(stays, mine, theirs), jnp.where(stays, theirs, mine)

    def join(self, kept, came):
        block = jnp.where(self.from_here(3)[self.core], kept, came)
        other = swap_cores(block)
        first = self.core == 0
        return jnp.stack([jnp.where(first, block, other), jnp.where(first, other, block)])


def on_device_scatter(
    amplitudes, slabs, couplings, occ_energy, vir_energy, occ_irrep, pair_i, pair_j, window_k, owner
):
    betas, block = slabs.shape[1], slabs.shape[3]
    windows = window_k.shape[0]
    rows = block // lax.axis_size("irrep")
    share = rows * block
    chips = lax.axis_size("pair")
    local_pairs = pair_i.shape[0]
    pairs = chips * local_pairs
    groups = pairs // GROUP
    lanes, depth, starts = tile_plan(rows)
    me, core = lax.axis_index("pair"), lax.axis_index("irrep")
    gamma, m = me & 1, me >> 1
    k_irrep = occ_irrep[window_k]
    bf16 = jnp.bfloat16

    chunks = b_chunks(block)
    local = slabs[0, :, 0]
    path = SlabPath(owner, k_irrep, me, core)
    kept_x, sent_x = zip(
        *[path.split_cores(local[:, :, first * block : (first + size) * block]) for first, size in chunks]
    )
    x, leaving_x = [], []
    for leaving in sent_x:
        leaving_x.append(after(leaving, x[-1]) if x else leaving)
        x.append(across(leaving_x[-1], 1))
    kept_y, sent_y, kept_z, sent_z, kept_h, sent_h = {}, {}, {}, {}, {}, {}
    y, z, h, ready = {}, {}, {}, {}

    def to_low(chunk, *tokens):
        kept_y[chunk], sent_y[chunk] = path.split_low(kept_x[chunk], after(x[chunk], *tokens))
        y[chunk] = across(sent_y[chunk], 2)

    def to_high(chunk, *tokens):
        kept_z[chunk], sent_z[chunk] = path.split_high(kept_y[chunk], after(y[chunk], *tokens))
        z[chunk] = across(sent_z[chunk], 4)

    def to_top(chunk, *tokens):
        kept_h[chunk], sent_h[chunk] = path.split_top(kept_z[chunk], after(z[chunk], *tokens))
        h[chunk] = across(sent_h[chunk], 8)

    def arrive(chunk, *tokens):
        ready[chunk] = path.join(kept_h[chunk], after(h[chunk], *tokens))

    to_low(0, sent_x[0])
    to_low(1, sent_y[0])
    to_high(0, sent_y[1])

    pair_sym = occ_irrep[pair_i] ^ occ_irrep[pair_j]
    mine = lax.dynamic_slice_in_dim(after(amplitudes, sent_x[0]), core * share, share, 2)
    target = jnp.arange(chips, dtype=jnp.int32)
    wanted = jnp.stack([target >> 1] + [(target >> 1) ^ (target & 1) ^ k_irrep[w] for w in range(windows)], 1)
    index = wanted[:, :, None] ^ pair_sym[None, None, :]
    kinds = 1 + windows
    labels = jnp.concatenate([pair_i, pair_j]).astype(bf16)
    labels = jnp.pad(labels, (0, share - labels.shape[0]))[None]
    stored = jnp.concatenate([mine.reshape(local_pairs * betas, share), labels], 0)
    index = index + betas * jnp.arange(local_pairs, dtype=jnp.int32)
    index = index.reshape(chips, kinds * local_pairs)
    index = jnp.pad(index, ((0, 0), (0, 1)), constant_values=local_pairs * betas).reshape(-1)
    chosen = (index[:, None] == jnp.arange(stored.shape[0], dtype=jnp.int32)[None, :]).astype(bf16)
    sent = jnp.einsum("rh,hx->rx", chosen, stored)
    sent = sent.reshape(chips, kinds * local_pairs + 1, share)
    came = lax.all_to_all(sent, "pair", 0, 0, tiled=True)
    came = after(came, sent_z[0], leaving_x[2])
    came = came.reshape(chips * (kinds * local_pairs + 1), share)
    label_rows = after(target, leaving_x[1]) * (kinds * local_pairs + 1) + kinds * local_pairs
    both = came[label_rows][:, : 2 * local_pairs].astype(jnp.int32).reshape(chips, 2, local_pairs)
    both = both.transpose(1, 0, 2).reshape(2, pairs)

    numbers = jnp.arange(pairs, dtype=jnp.int32)
    ahead = both[0][None, :] < both[0][:, None]
    tied = (both[0][None, :] == both[0][:, None]) & (numbers[None, :] < numbers[:, None])
    rank = jnp.sum((ahead | tied).astype(jnp.int32), axis=1)
    placed = (rank[None, :] == numbers[:, None]).astype(jnp.int32)
    order = jnp.sum(placed * numbers[None, :], axis=1)
    first = jnp.sum(placed * both[0][None, :], axis=1)
    second = jnp.sum(placed * both[1][None, :], axis=1)

    source = (order // local_pairs) * (kinds * local_pairs + 1) + order % local_pairs
    source = source[None, :] + local_pairs * jnp.arange(kinds, dtype=jnp.int32)[:, None]
    amps = came[source]
    amps = amps.reshape(kinds, groups, GROUP, rows, block)
    holes = amps[1:]
    used = GROUP * rows
    at = amps[0].transpose(0, 3, 1, 2).reshape(groups, block, used)
    at = jnp.pad(at, ((0, 0), (0, LANE - block), (0, lanes - used)))
    lane = jnp.arange(lanes, dtype=jnp.int32)
    spread = ((lane[None, :] % rows == jnp.arange(rows)[:, None]) & (lane < used)[None, :]).astype(bf16)
    lane_pair = lane // rows
    mask = jnp.stack([
        (jnp.repeat(start + jnp.arange(depth), GROUP)[:, None] == lane_pair[None, n * TILE : (n + 1) * TILE])
        for n, start in enumerate(starts)
    ]).astype(bf16)

    coupled = jnp.where(gamma == core, couplings, swap_cores(couplings))
    chosen = (second.reshape(groups, GROUP)[:, :, None] == jnp.arange(occ_irrep.shape[0])).astype(bf16)
    coupled = jnp.einsum("gql,wljc->wgqjc", chosen, coupled)
    coupled = jnp.einsum("gpj,wgqjc->wgcpq", chosen, coupled)
    sym_j = occ_irrep[second].reshape(groups, GROUP)
    keep = (sym_j[None, :, :, None] ^ sym_j[None, :, None, :] ^ gamma ^ k_irrep[:, None, None, None]) == 0
    coupled = -(coupled * keep[:, :, None].astype(bf16))
    ct = jnp.stack(
        [coupled[:, :, :, s : s + depth].reshape(windows, groups, block, depth * GROUP) for s in starts], 2
    )

    alpha = occ_irrep[first] ^ occ_irrep[second] ^ m
    energy_a = lax.dynamic_slice_in_dim(vir_energy, core * rows, rows, 1)[alpha]
    base = occ_energy[first] + occ_energy[second]
    lrow = energy_a[None] - (base[None] + occ_energy[window_k][:, None])[:, :, None]
    lrow = lrow.reshape(windows, groups, 1, used)
    lrow = jnp.pad(lrow, ((0, 0), (0, 0), (0, 0), (0, lanes - used)), constant_values=1.0)
    ecol = jnp.broadcast_to(pick(vir_energy, gamma)[:, None], (block, TILE))
    energy_b = vir_energy[m ^ gamma ^ k_irrep]

    eye = (jnp.arange(block)[:, None] == jnp.arange(LANE)[None, :]).astype(bf16)

    def spread_holes(chunk, *tokens):
        start, size = chunks[chunk]
        hole = after(holes[:, :, :, :, start : start + size], *tokens)
        return jnp.einsum("wgqab,ae->wgbqe", hole, spread)

    def run(chunk, w, v, total):
        start, size = chunks[chunk]
        vt = jnp.einsum("wdx,de->wxe", v, eye).reshape(windows, size, block, LANE)
        last = start + size == block and w == windows - 1
        energies = energy_b[:, start : start + size]
        return triples_call(w, last, energies, vt, v, at, areps[chunk], ct, mask, ecol, lrow, total)

    calls = [(chunk, w) for chunk in range(len(chunks)) for w in range(windows)]
    to_top(0, amps)
    to_high(1, sent_h[0])
    to_low(2, sent_z[1])
    at = after(at, sent_y[2], leaving_x[3])
    areps = {0: spread_holes(0, at)}
    ct = after(ct, areps[0])
    arrive(0, ct)
    to_top(1, ready[0])
    ready[0] = after(ready[0], sent_h[1])
    total = None
    for n, (chunk, w) in enumerate(calls):
        total = run(chunk, w, ready[chunk], total)
        if n == 0:
            arrive(1, total)
            areps[1] = spread_holes(1, total)
            total = after(total, ready[1])
        elif n == 1:
            to_high(2, total)
            to_low(3, sent_z[2])
            total = after(total, sent_y[3])
        elif n == 2:
            to_top(2, total)
            total = after(total, sent_h[2])
        elif n == 3:
            areps[2] = spread_holes(2, total)
            areps[3] = spread_holes(3, areps[2])
            to_high(3, areps[3])
            arrive(2, sent_z[3])
        elif n == 4:
            to_top(3, total)
            total = after(total, sent_h[3])
        elif n == 5:
            arrive(3, total)
    total = total[:, :used].reshape(pairs, share)[rank]
    cut = 8 if share % 8 == 0 else 1
    total = total.reshape(chips, local_pairs * cut, share // cut)
    came = lax.all_to_all(total, "pair", 0, 0, tiled=True)
    came = came.reshape(betas, 2, local_pairs, cut, share // cut)
    came = (came[:, 0] + came[:, 1]).reshape(betas, local_pairs, share)
    back = jnp.arange(betas, dtype=jnp.int32)[None, :] ^ pair_sym[:, None]
    return came[back, jnp.arange(local_pairs, dtype=jnp.int32)[:, None]]


def on_device(*args):
    betas, block = args[1].shape[1], args[1].shape[3]
    chips, cores = lax.axis_size("pair"), lax.axis_size("irrep")
    fits = lax.axis_size("vtile") == 1 and cores == 2 and betas == 8 and chips == betas * cores
    fits = fits and args[8].shape[0] == 2 and block % 2 == 0 and block < LANE
    fits = fits and all(size > 0 and size % 2 == 0 for _, size in b_chunks(block))
    if fits and args[5].shape[0] <= 256:
        return on_device_scatter(*args)
    return on_device_gather(*args)


def solution(mesh):
    placed = (
        P("pair", None, None),
        P("pair", "vtile", "irrep", None, None),
        P(None, None, None, "irrep"),
        P(),
        P(),
        P(),
        P("pair"),
        P("pair"),
        P(),
        P(),
    )
    return jax.shard_map(
        on_device,
        mesh=mesh,
        in_specs=placed,
        out_specs=P("pair", "vtile", "irrep"),
        check_vma=False,
    )
```

```python
import functools
import math

import jax
import jax.numpy as jnp
from jax import lax
from jax.experimental import pallas as pl
from jax.experimental.pallas import tpu as pltpu
from jax.sharding import PartitionSpec as P


K_WIN = 2


def spread_2(shard, axis, root):
    mine = lax.axis_index(axis) == root
    return lax.psum(jnp.where(mine, shard, jnp.zeros_like(shard)), axis)


def on_device_gather(
    amplitudes, slabs, couplings, occ_energy, vir_energy, occ_irrep, pair_i, pair_j, window_k, owner
):
    tile_blocks = slabs.shape[1]
    block_size = slabs.shape[3]
    block_area = block_size * block_size
    occ_count = occ_irrep.shape[0]
    local_pairs = amplitudes.shape[0]
    tile_index = lax.axis_index("vtile")
    gamma_irrep = lax.axis_index("irrep")
    beta_irreps = tile_index * tile_blocks + jnp.arange(tile_blocks, dtype=jnp.int32)
    pair_sym = jnp.bitwise_xor(occ_irrep[pair_i], occ_irrep[pair_j])
    send_index = jnp.bitwise_xor(beta_irreps[None, :], pair_sym[:, None])
    outgoing = jnp.take_along_axis(amplitudes, send_index[:, :, None], axis=1)
    local_slab = slabs[0, :, 0]
    gamma_energy = jnp.take(vir_energy, gamma_irrep, axis=0)
    beta_energy = vir_energy[beta_irreps]
    occ_keep = jnp.bitwise_xor(occ_irrep, gamma_irrep)

    def pair_term(amp_pair, occ_i, occ_j, hole_part, slab_data, k_irrep, k_energy):
        pair_irrep = jnp.bitwise_xor(occ_irrep[occ_i], occ_irrep[occ_j])
        alpha_irrep = jnp.bitwise_xor(
            jnp.bitwise_xor(pair_irrep, k_irrep), jnp.bitwise_xor(beta_irreps, gamma_irrep)
        )
        amp_sel = amp_pair[alpha_irrep].reshape(tile_blocks, block_size, block_size)
        particle = jnp.einsum(
            "mad,mdx->max", amp_sel, slab_data, preferred_element_type=jnp.float32
        )
        energy_a = vir_energy[alpha_irrep]
        base = occ_energy[occ_i] + occ_energy[occ_j] + k_energy
        denominator = (
            energy_a[:, :, None, None]
            + beta_energy[:, None, :, None]
            + gamma_energy[None, None, None, :]
            - base
        )
        triples = (
            (particle - hole_part) / denominator.reshape(tile_blocks, block_size, block_area)
        ).astype(jnp.bfloat16)
        contrib = jnp.einsum("max,mdx->mad", triples, slab_data, preferred_element_type=jnp.float32)
        return (
            jnp.zeros((8, block_area), jnp.float32)
            .at[alpha_irrep]
            .add(contrib.reshape(tile_blocks, block_area))
        )

    def coupling_rows(window, occ_j, k_irrep):
        y_column = jnp.take(couplings[window], occ_j, axis=1)
        keep_mask = jnp.bitwise_xor(occ_keep, jnp.bitwise_xor(occ_irrep[occ_j], k_irrep)) == 0
        return y_column.astype(jnp.float32) * keep_mask[:, None].astype(jnp.float32)

    empty_stash = jnp.zeros((local_pairs, occ_count, tile_blocks, block_area), jnp.bfloat16)
    empty_seen = jnp.zeros((local_pairs, occ_count), jnp.float32)
    stash = empty_stash
    seen = empty_seen
    piece_amp = lax.all_gather(outgoing, "pair", axis=0, tiled=True)
    piece_first = lax.all_gather(pair_i, "pair", axis=0, tiled=True)
    piece_second = lax.all_gather(pair_j, "pair", axis=0, tiled=True)
    match = piece_first[None, :] == pair_i[:, None]
    slot = jnp.where(match, piece_second[None, :], occ_count).astype(jnp.int32)
    row_index = jnp.broadcast_to(jnp.arange(local_pairs, dtype=jnp.int32)[:, None], slot.shape)
    spread = jnp.broadcast_to(piece_amp[None], (local_pairs,) + piece_amp.shape)
    stash = stash.at[row_index, slot].add(spread, mode="drop")
    seen = seen.at[row_index, slot].add(jnp.ones(slot.shape, jnp.float32), mode="drop")
    accumulated = jnp.zeros((local_pairs, 8, block_area), jnp.float32)
    for window in range(K_WIN):
        slab_data = spread_2(local_slab, "pair", owner[window])
        k_index = window_k[window]
        k_irrep = occ_irrep[k_index]
        k_energy = occ_energy[k_index]

        def folded_step(packed):
            amp_pair, occ_i, occ_j, slot_amp, slot_seen = packed
            coef_rows = coupling_rows(window, occ_j, k_irrep)
            coupling = (coef_rows * slot_seen[:, None]).astype(jnp.bfloat16)
            hole_part = jnp.einsum(
                "qmx,qc->mxc", slot_amp, coupling, preferred_element_type=jnp.float32
            )
            hole_part = hole_part.reshape(tile_blocks, block_size, block_area)
            return pair_term(amp_pair, occ_i, occ_j, hole_part, slab_data, k_irrep, k_energy)

        contrib_all = lax.map(folded_step, (amplitudes, pair_i, pair_j, stash, seen))
        accumulated = accumulated + contrib_all
    summed = lax.psum(accumulated, ("vtile", "irrep"))
    irrep_count = lax.axis_size("irrep")
    share = block_area // irrep_count
    summed = lax.dynamic_slice_in_dim(summed, tile_index * tile_blocks, tile_blocks, 1)
    return lax.dynamic_slice_in_dim(summed, gamma_irrep * share, share, 2)


GROUP = 16
LANE = 128
TILE = 256
STEP = 8


def tile_plan(rows):
    lanes = -(-GROUP * rows // TILE) * TILE
    depth = LANE // GROUP
    starts = []
    for first in range(0, lanes, TILE):
        lowest = min(first // rows, GROUP - depth)
        highest = min((first + TILE - 1) // rows, GROUP - 1)
        assert lowest >= 0 and highest < lowest + depth
        starts.append(lowest)
    return lanes, depth, starts


def b_chunks(block):
    unit = LANE // math.gcd(LANE, block)
    sizes = (unit, unit, 2 * unit, block - 4 * unit)
    return [(sum(sizes[:n]), size) for n, size in enumerate(sizes)]


def triples_kernel(last, *refs):
    eb_ref, vt_ref, v_ref, at_ref, arep_ref, ct_ref, mask_ref, ecol_ref, lrow_ref = refs[:9]
    o_ref, t_ref = refs[-2:]
    count, block = vt_ref.shape[1], vt_ref.shape[2]
    unroll = math.gcd(count, STEP)
    depth = mask_ref.shape[1] // GROUP
    tiles = mask_ref.shape[0]

    def some_b(step, carry):
        for tile in range(tiles):
            lanes = slice(tile * TILE, (tile + 1) * TILE)
            top = at_ref[0, :, lanes]
            for first in range(0, unroll, 2):
                results = []
                for b in (unroll * step + first, unroll * step + first + 1):
                    lhs = jnp.concatenate([vt_ref[0, b], ct_ref[0, 0, tile]], axis=1)
                    hole_amp = arep_ref[0, 0, b, :, lanes]
                    bottom = jnp.concatenate([hole_amp] * depth, axis=0) * mask_ref[tile]
                    rhs = jnp.concatenate([top, bottom], axis=0)
                    numer = jnp.dot(lhs, rhs, preferred_element_type=jnp.float32)
                    denom = (ecol_ref[...] + eb_ref[0, b]) + lrow_ref[0, 0, :, lanes]
                    results.append(numer / denom)
                start = pl.multiple_of((unroll * step + first) * block, 2 * block)
                t_ref[pl.ds(start, 2 * block), lanes] = jnp.concatenate(results, axis=0).astype(jnp.bfloat16)
        return carry

    lax.fori_loop(0, count // unroll, some_b, 0)

    def finish(tile, carry):
        lanes = pl.ds(pl.multiple_of(tile * TILE, TILE), TILE)
        contrib = jnp.dot(v_ref[0], t_ref[:, lanes], preferred_element_type=jnp.float32)
        if len(refs) == 12:
            contrib = contrib + refs[9][0, :, lanes]
        if last:
            o_ref[0, lanes, :] = contrib.T
        else:
            o_ref[0, :, lanes] = contrib
        return carry

    lax.fori_loop(0, tiles, finish, 0)


def triples_call(window, last, eb, vt, v, at, arep, ct, mask, ecol, lrow, total=None):
    _, count, block, _ = vt.shape
    groups, depth_rows, lanes = at.shape
    w = window
    tall, wide = pl.BlockSpec((1, lanes, block), lambda g: (g, 0, 0)), pl.BlockSpec((1, block, lanes), lambda g: (g, 0, 0))
    in_specs = [
        pl.BlockSpec(memory_space=pltpu.SMEM),
        pl.BlockSpec((1, count, block, LANE), lambda g: (w, 0, 0, 0)),
        pl.BlockSpec((1, block, count * block), lambda g: (w, 0, 0)),
        pl.BlockSpec((1, depth_rows, lanes), lambda g: (g, 0, 0)),
        pl.BlockSpec((1, 1, count, GROUP, lanes), lambda g: (w, g, 0, 0, 0)),
        pl.BlockSpec((1, 1) + ct.shape[2:], lambda g: (w, g, 0, 0, 0)),
        pl.BlockSpec(mask.shape, lambda g: (0, 0, 0)),
        pl.BlockSpec(ecol.shape, lambda g: (0, 0)),
        pl.BlockSpec((1, 1, 1, lanes), lambda g: (w, g, 0, 0)),
    ]
    operands = [eb[w : w + 1], vt, v, at, arep, ct, mask, ecol, lrow]
    if total is not None:
        in_specs.append(wide)
        operands.append(total)
    shape = (groups, lanes, block) if last else (groups, block, lanes)
    return pl.pallas_call(
        functools.partial(triples_kernel, last),
        grid=(groups,),
        in_specs=in_specs,
        out_specs=tall if last else wide,
        out_shape=jax.ShapeDtypeStruct(shape, jnp.float32),
        scratch_shapes=[pltpu.VMEM((count * block, lanes), jnp.bfloat16)],
        compiler_params=pltpu.CompilerParams(
            dimension_semantics=("arbitrary",), vmem_limit_bytes=40 * 1024 * 1024
        ),
        cost_estimate=pl.CostEstimate(
            flops=groups * count * block * lanes * 2 * (TILE + block) * 4,
            bytes_accessed=(arep.size + vt.size + v.size) * 2,
            transcendentals=groups * count * block * lanes,
        ),
        name="triples",
    )(*operands)


def swap_cores(x):
    return lax.ppermute(x, "irrep", [(0, 1), (1, 0)])


def across(x, bit):
    count = lax.axis_size("pair")
    return lax.ppermute(x, "pair", [(t, t ^ bit) for t in range(count)])


def pick(x, index):
    return lax.dynamic_index_in_dim(x, index, 0, keepdims=False)


def after(x, *others):
    return lax.optimization_barrier((x,) + others)[0]


class SlabPath:
    def __init__(self, owner, k_irrep, me, core):
        self.owner, self.k_irrep, self.core = owner, k_irrep, core
        self.windows = owner.shape[0]
        self.bits = [(me >> n) & 1 for n in range(4)]

    def from_here(self, bit):
        return ((self.owner >> bit) & 1) == self.bits[bit]

    def split_cores(self, slab):
        halves = slab.reshape((2, slab.shape[0] // 2) + slab.shape[1:])
        mine, theirs = pick(halves, self.core), swap_cores(pick(halves, 1 - self.core))
        same = self.bits[0] == self.core
        return jnp.where(same, mine, theirs), jnp.where(same, theirs, mine)

    def split_low(self, kept, came):
        def block(w, high, low):
            beta = (2 * high + low) ^ (self.k_irrep[w] & 3) ^ self.bits[0]
            return jnp.where(self.from_here(0)[w], pick(kept, beta), pick(came, beta))

        def blocks(low):
            return jnp.stack(
                [jnp.stack([block(w, high, low) for w in range(self.windows)]) for high in range(2)]
            )

        return blocks(self.bits[1]), blocks(1 - self.bits[1])

    def split_high(self, kept, came):
        here = self.from_here(1)[:, None, None]
        kept, leaving = [
            jnp.where(here, pick(kept, high), pick(came, high)) for high in (self.bits[2], 1 - self.bits[2])
        ]
        return kept, leaving

    def split_top(self, kept, came):
        blocks = jnp.where(self.from_here(2)[:, None, None], kept, came)
        mine, theirs = pick(blocks, self.core), swap_cores(pick(blocks, 1 - self.core))
        stays = (self.bits[3] ^ ((self.k_irrep[self.core] >> 2) & 1)) == self.core
        return jnp.where(stays, mine, theirs), jnp.where(stays, theirs, mine)

    def join(self, kept, came):
        block = jnp.where(self.from_here(3)[self.core], kept, came)
        other = swap_cores(block)
        first = self.core == 0
        return jnp.stack([jnp.where(first, block, other), jnp.where(first, other, block)])


def on_device_scatter(
    amplitudes, slabs, couplings, occ_energy, vir_energy, occ_irrep, pair_i, pair_j, window_k, owner
):
    betas, block = slabs.shape[1], slabs.shape[3]
    windows = window_k.shape[0]
    rows = block // lax.axis_size("irrep")
    share = rows * block
    chips = lax.axis_size("pair")
    local_pairs = pair_i.shape[0]
    pairs = chips * local_pairs
    groups = pairs // GROUP
    lanes, depth, starts = tile_plan(rows)
    me, core = lax.axis_index("pair"), lax.axis_index("irrep")
    gamma, m = me & 1, me >> 1
    k_irrep = occ_irrep[window_k]
    bf16 = jnp.bfloat16

    chunks = b_chunks(block)
    local = slabs[0, :, 0]
    path = SlabPath(owner, k_irrep, me, core)
    labels = jnp.pad(jnp.concatenate([pair_i, pair_j]), (0, LANE - 2 * local_pairs))
    labels = lax.all_to_all(jnp.broadcast_to(labels, (chips, 1, LANE)), "pair", 0, 0, tiled=True)
    kept_x, sent_x = zip(
        *[path.split_cores(local[:, :, first * block : (first + size) * block]) for first, size in chunks]
    )
    x, leaving_x = [], []
    for leaving in sent_x:
        leaving_x.append(after(leaving, x[-1]) if x else leaving)
        x.append(across(leaving_x[-1], 1))
    kept_y, sent_y, kept_z, sent_z, kept_h, sent_h = {}, {}, {}, {}, {}, {}
    y, z, h, ready = {}, {}, {}, {}

    def to_low(chunk, *tokens):
        kept_y[chunk], sent_y[chunk] = path.split_low(kept_x[chunk], after(x[chunk], *tokens))
        y[chunk] = across(sent_y[chunk], 2)

    def to_high(chunk, *tokens):
        kept_z[chunk], sent_z[chunk] = path.split_high(kept_y[chunk], after(y[chunk], *tokens))
        z[chunk] = across(sent_z[chunk], 4)

    def to_top(chunk, *tokens):
        kept_h[chunk], sent_h[chunk] = path.split_top(kept_z[chunk], after(z[chunk], *tokens))
        h[chunk] = across(sent_h[chunk], 8)

    def arrive(chunk, *tokens):
        ready[chunk] = path.join(kept_h[chunk], after(h[chunk], *tokens))

    to_low(0, sent_x[0])
    to_low(1, sent_y[0])
    to_high(0, sent_y[1])

    pair_sym = occ_irrep[pair_i] ^ occ_irrep[pair_j]
    mine = lax.dynamic_slice_in_dim(after(amplitudes, sent_x[0]), core * share, share, 2)
    target = jnp.arange(chips, dtype=jnp.int32)
    wanted = jnp.stack([target >> 1] + [(target >> 1) ^ (target & 1) ^ k_irrep[w] for w in range(windows)], 1)
    index = wanted[:, :, None] ^ pair_sym[None, None, :]
    kinds = 1 + windows
    stored = mine.reshape(local_pairs * betas, share)
    index = index + betas * jnp.arange(local_pairs, dtype=jnp.int32)
    index = jnp.pad(index.reshape(chips, -1), ((0, 0), (0, 1)), constant_values=-1).reshape(-1)
    chosen = (index[:, None] == jnp.arange(stored.shape[0], dtype=jnp.int32)[None, :]).astype(bf16)
    sent = jnp.einsum("rh,hx->rx", chosen, stored)
    sent = sent.reshape(chips, kinds * local_pairs + 1, share)
    came = lax.all_to_all(sent, "pair", 0, 0, tiled=True)

    labels = after(labels, sent)
    both = labels[:, 0, : 2 * local_pairs]
    both = both.reshape(chips, 2, local_pairs).transpose(1, 0, 2).reshape(2, pairs)
    numbers = jnp.arange(pairs, dtype=jnp.int32)
    ahead = both[0][None, :] < both[0][:, None]
    tied = (both[0][None, :] == both[0][:, None]) & (numbers[None, :] < numbers[:, None])
    rank = jnp.sum((ahead | tied).astype(jnp.int32), axis=1)
    placed = (rank[None, :] == numbers[:, None]).astype(jnp.int32)
    order = jnp.sum(placed * numbers[None, :], axis=1)
    first = jnp.sum(placed * both[0][None, :], axis=1)
    second = jnp.sum(placed * both[1][None, :], axis=1)

    used = GROUP * rows
    coupled = jnp.where(gamma == core, couplings, swap_cores(couplings))
    chosen = (second.reshape(groups, GROUP)[:, :, None] == jnp.arange(occ_irrep.shape[0])).astype(bf16)
    coupled = jnp.einsum("gql,wljc->wgqjc", chosen, coupled)
    coupled = jnp.einsum("gpj,wgqjc->wgcpq", chosen, coupled)
    sym_j = occ_irrep[second].reshape(groups, GROUP)
    keep = (sym_j[None, :, :, None] ^ sym_j[None, :, None, :] ^ gamma ^ k_irrep[:, None, None, None]) == 0
    coupled = -(coupled * keep[:, :, None].astype(bf16))
    ct = jnp.stack(
        [coupled[:, :, :, s : s + depth].reshape(windows, groups, block, depth * GROUP) for s in starts], 2
    )

    alpha = occ_irrep[first] ^ occ_irrep[second] ^ m
    energy_a = lax.dynamic_slice_in_dim(vir_energy, core * rows, rows, 1)[alpha]
    base = occ_energy[first] + occ_energy[second]
    lrow = energy_a[None] - (base[None] + occ_energy[window_k][:, None])[:, :, None]
    lrow = lrow.reshape(windows, groups, 1, used)
    lrow = jnp.pad(lrow, ((0, 0), (0, 0), (0, 0), (0, lanes - used)), constant_values=1.0)
    source = (order // local_pairs) * (kinds * local_pairs + 1) + order % local_pairs
    source = source[None, :] + local_pairs * jnp.arange(kinds, dtype=jnp.int32)[:, None]
    came = after(came, sent_z[0], leaving_x[2], ct, lrow, source)
    came = came.reshape(chips * (kinds * local_pairs + 1), share)
    amps = came[source]
    amps = amps.reshape(kinds, groups, GROUP, rows, block)
    holes = lax.optimization_barrier(amps[1:].transpose(0, 1, 4, 2, 3))
    at = amps[0].transpose(0, 3, 1, 2).reshape(groups, block, used)
    at = jnp.pad(at, ((0, 0), (0, LANE - block), (0, lanes - used)))
    lane = jnp.arange(lanes, dtype=jnp.int32)
    spread = ((lane[None, :] % rows == jnp.arange(rows)[:, None]) & (lane < used)[None, :]).astype(bf16)
    lane_pair = lane // rows
    mask = jnp.stack([
        (jnp.repeat(start + jnp.arange(depth), GROUP)[:, None] == lane_pair[None, n * TILE : (n + 1) * TILE])
        for n, start in enumerate(starts)
    ]).astype(bf16)

    ecol = jnp.broadcast_to(pick(vir_energy, gamma)[:, None], (block, TILE))
    energy_b = vir_energy[m ^ gamma ^ k_irrep]

    eye = (jnp.arange(block)[:, None] == jnp.arange(LANE)[None, :]).astype(bf16)

    def spread_holes(chunk, *tokens):
        start, size = chunks[chunk]
        hole = after(holes, *tokens)[:, :, start : start + size]
        return jnp.einsum("wgbqa,ae->wgbqe", hole, spread)

    def run(chunk, w, v, total):
        start, size = chunks[chunk]
        vt = jnp.einsum("wdx,de->wxe", v, eye).reshape(windows, size, block, LANE)
        last = start + size == block and w == windows - 1
        energies = energy_b[:, start : start + size]
        return triples_call(w, last, energies, vt, v, at, areps[chunk], ct, mask, ecol, lrow, total)

    calls = [(chunk, w) for chunk in range(len(chunks)) for w in range(windows)]
    to_top(0, amps)
    to_high(1, sent_h[0])
    to_low(2, sent_z[1])
    at = after(at, sent_y[2], leaving_x[3])
    areps = {0: spread_holes(0, at)}
    ct = after(ct, areps[0])
    arrive(0, ct)
    to_top(1, ready[0])
    ready[0] = after(ready[0], sent_h[1])
    total = None
    for n, (chunk, w) in enumerate(calls):
        total = run(chunk, w, ready[chunk], total)
        if n == 0:
            arrive(1, total)
            areps[1] = spread_holes(1, total)
            total = after(total, ready[1])
        elif n == 1:
            to_high(2, total)
            to_low(3, sent_z[2])
            total = after(total, sent_y[3])
        elif n == 2:
            to_top(2, total)
            total = after(total, sent_h[2])
        elif n == 3:
            areps[2] = spread_holes(2, total)
            areps[3] = spread_holes(3, areps[2])
            to_high(3, areps[3])
            arrive(2, sent_z[3])
        elif n == 4:
            to_top(3, total)
            total = after(total, sent_h[3])
        elif n == 5:
            arrive(3, total)
    total = total[:, :used].reshape(pairs, share)[rank]
    cut = 8 if share % 8 == 0 else 1
    total = total.reshape(chips, local_pairs * cut, share // cut)
    came = lax.all_to_all(total, "pair", 0, 0, tiled=True)
    came = came.reshape(betas, 2, local_pairs, cut, share // cut)
    came = (came[:, 0] + came[:, 1]).reshape(betas, local_pairs, share)
    back = jnp.arange(betas, dtype=jnp.int32)[None, :] ^ pair_sym[:, None]
    return came[back, jnp.arange(local_pairs, dtype=jnp.int32)[:, None]]


def on_device(*args):
    betas, block = args[1].shape[1], args[1].shape[3]
    chips, cores = lax.axis_size("pair"), lax.axis_size("irrep")
    fits = lax.axis_size("vtile") == 1 and cores == 2 and betas == 8 and chips == betas * cores
    fits = fits and args[8].shape[0] == 2 and block % 2 == 0 and block < LANE
    fits = fits and all(size > 0 and size % 2 == 0 for _, size in b_chunks(block))
    if fits and 2 * args[6].shape[0] <= LANE:
        return on_device_scatter(*args)
    return on_device_gather(*args)


def solution(mesh):
    placed = (
        P("pair", None, None),
        P("pair", "vtile", "irrep", None, None),
        P(None, None, None, "irrep"),
        P(),
        P(),
        P(),
        P("pair"),
        P("pair"),
        P(),
        P(),
    )
    return jax.shard_map(
        on_device,
        mesh=mesh,
        in_specs=placed,
        out_specs=P("pair", "vtile", "irrep"),
        check_vma=False,
    )
```

```python
import functools
import math

import jax
import jax.numpy as jnp
from jax import lax
from jax.experimental import pallas as pl
from jax.experimental.pallas import tpu as pltpu
from jax.sharding import PartitionSpec as P


K_WIN = 2


def spread_2(shard, axis, root):
    mine = lax.axis_index(axis) == root
    return lax.psum(jnp.where(mine, shard, jnp.zeros_like(shard)), axis)


def on_device_gather(
    amplitudes, slabs, couplings, occ_energy, vir_energy, occ_irrep, pair_i, pair_j, window_k, owner
):
    tile_blocks = slabs.shape[1]
    block_size = slabs.shape[3]
    block_area = block_size * block_size
    occ_count = occ_irrep.shape[0]
    local_pairs = amplitudes.shape[0]
    tile_index = lax.axis_index("vtile")
    gamma_irrep = lax.axis_index("irrep")
    beta_irreps = tile_index * tile_blocks + jnp.arange(tile_blocks, dtype=jnp.int32)
    pair_sym = jnp.bitwise_xor(occ_irrep[pair_i], occ_irrep[pair_j])
    send_index = jnp.bitwise_xor(beta_irreps[None, :], pair_sym[:, None])
    outgoing = jnp.take_along_axis(amplitudes, send_index[:, :, None], axis=1)
    local_slab = slabs[0, :, 0]
    gamma_energy = jnp.take(vir_energy, gamma_irrep, axis=0)
    beta_energy = vir_energy[beta_irreps]
    occ_keep = jnp.bitwise_xor(occ_irrep, gamma_irrep)

    def pair_term(amp_pair, occ_i, occ_j, hole_part, slab_data, k_irrep, k_energy):
        pair_irrep = jnp.bitwise_xor(occ_irrep[occ_i], occ_irrep[occ_j])
        alpha_irrep = jnp.bitwise_xor(
            jnp.bitwise_xor(pair_irrep, k_irrep), jnp.bitwise_xor(beta_irreps, gamma_irrep)
        )
        amp_sel = amp_pair[alpha_irrep].reshape(tile_blocks, block_size, block_size)
        particle = jnp.einsum(
            "mad,mdx->max", amp_sel, slab_data, preferred_element_type=jnp.float32
        )
        energy_a = vir_energy[alpha_irrep]
        base = occ_energy[occ_i] + occ_energy[occ_j] + k_energy
        denominator = (
            energy_a[:, :, None, None]
            + beta_energy[:, None, :, None]
            + gamma_energy[None, None, None, :]
            - base
        )
        triples = (
            (particle - hole_part) / denominator.reshape(tile_blocks, block_size, block_area)
        ).astype(jnp.bfloat16)
        contrib = jnp.einsum("max,mdx->mad", triples, slab_data, preferred_element_type=jnp.float32)
        return (
            jnp.zeros((8, block_area), jnp.float32)
            .at[alpha_irrep]
            .add(contrib.reshape(tile_blocks, block_area))
        )

    def coupling_rows(window, occ_j, k_irrep):
        y_column = jnp.take(couplings[window], occ_j, axis=1)
        keep_mask = jnp.bitwise_xor(occ_keep, jnp.bitwise_xor(occ_irrep[occ_j], k_irrep)) == 0
        return y_column.astype(jnp.float32) * keep_mask[:, None].astype(jnp.float32)

    empty_stash = jnp.zeros((local_pairs, occ_count, tile_blocks, block_area), jnp.bfloat16)
    empty_seen = jnp.zeros((local_pairs, occ_count), jnp.float32)
    stash = empty_stash
    seen = empty_seen
    piece_amp = lax.all_gather(outgoing, "pair", axis=0, tiled=True)
    piece_first = lax.all_gather(pair_i, "pair", axis=0, tiled=True)
    piece_second = lax.all_gather(pair_j, "pair", axis=0, tiled=True)
    match = piece_first[None, :] == pair_i[:, None]
    slot = jnp.where(match, piece_second[None, :], occ_count).astype(jnp.int32)
    row_index = jnp.broadcast_to(jnp.arange(local_pairs, dtype=jnp.int32)[:, None], slot.shape)
    spread = jnp.broadcast_to(piece_amp[None], (local_pairs,) + piece_amp.shape)
    stash = stash.at[row_index, slot].add(spread, mode="drop")
    seen = seen.at[row_index, slot].add(jnp.ones(slot.shape, jnp.float32), mode="drop")
    accumulated = jnp.zeros((local_pairs, 8, block_area), jnp.float32)
    for window in range(K_WIN):
        slab_data = spread_2(local_slab, "pair", owner[window])
        k_index = window_k[window]
        k_irrep = occ_irrep[k_index]
        k_energy = occ_energy[k_index]

        def folded_step(packed):
            amp_pair, occ_i, occ_j, slot_amp, slot_seen = packed
            coef_rows = coupling_rows(window, occ_j, k_irrep)
            coupling = (coef_rows * slot_seen[:, None]).astype(jnp.bfloat16)
            hole_part = jnp.einsum(
                "qmx,qc->mxc", slot_amp, coupling, preferred_element_type=jnp.float32
            )
            hole_part = hole_part.reshape(tile_blocks, block_size, block_area)
            return pair_term(amp_pair, occ_i, occ_j, hole_part, slab_data, k_irrep, k_energy)

        contrib_all = lax.map(folded_step, (amplitudes, pair_i, pair_j, stash, seen))
        accumulated = accumulated + contrib_all
    summed = lax.psum(accumulated, ("vtile", "irrep"))
    irrep_count = lax.axis_size("irrep")
    share = block_area // irrep_count
    summed = lax.dynamic_slice_in_dim(summed, tile_index * tile_blocks, tile_blocks, 1)
    return lax.dynamic_slice_in_dim(summed, gamma_irrep * share, share, 2)


GROUP = 16
LANE = 128
TILE = 256
STEP = 8


def tile_plan(rows):
    lanes = -(-GROUP * rows // TILE) * TILE
    depth = LANE // GROUP
    starts = []
    for first in range(0, lanes, TILE):
        lowest = min(first // rows, GROUP - depth)
        highest = min((first + TILE - 1) // rows, GROUP - 1)
        assert lowest >= 0 and highest < lowest + depth
        starts.append(lowest)
    return lanes, depth, starts


def b_chunks(block):
    unit = LANE // math.gcd(LANE, block)
    sizes = (unit, unit, 2 * unit, block - 4 * unit)
    return [(sum(sizes[:n]), size) for n, size in enumerate(sizes)]


def triples_kernel(last, *refs):
    eb_ref, vt_ref, v_ref, at_ref, arep_ref, ct_ref, mask_ref, ecol_ref, lrow_ref = refs[:9]
    o_ref, t_ref = refs[-2:]
    count, block = vt_ref.shape[1], vt_ref.shape[2]
    unroll = math.gcd(count, STEP)
    depth = mask_ref.shape[1] // GROUP
    tiles = mask_ref.shape[0]

    def some_b(step, carry):
        for tile in range(tiles):
            lanes = slice(tile * TILE, (tile + 1) * TILE)
            top = at_ref[0, :, lanes]
            for first in range(0, unroll, 2):
                results = []
                for b in (unroll * step + first, unroll * step + first + 1):
                    lhs = jnp.concatenate([vt_ref[0, b], ct_ref[0, 0, tile]], axis=1)
                    hole_amp = arep_ref[0, 0, b, :, lanes]
                    bottom = jnp.concatenate([hole_amp] * depth, axis=0) * mask_ref[tile]
                    rhs = jnp.concatenate([top, bottom], axis=0)
                    numer = jnp.dot(lhs, rhs, preferred_element_type=jnp.float32)
                    denom = (ecol_ref[...] + eb_ref[0, b]) + lrow_ref[0, 0, :, lanes]
                    results.append(numer / denom)
                start = pl.multiple_of((unroll * step + first) * block, 2 * block)
                t_ref[pl.ds(start, 2 * block), lanes] = jnp.concatenate(results, axis=0).astype(jnp.bfloat16)
        return carry

    lax.fori_loop(0, count // unroll, some_b, 0)

    def finish(tile, carry):
        lanes = pl.ds(pl.multiple_of(tile * TILE, TILE), TILE)
        contrib = jnp.dot(v_ref[0], t_ref[:, lanes], preferred_element_type=jnp.float32)
        if len(refs) == 12:
            contrib = contrib + refs[9][0, :, lanes]
        if last:
            o_ref[0, lanes, :] = contrib.T
        else:
            o_ref[0, :, lanes] = contrib
        return carry

    lax.fori_loop(0, tiles, finish, 0)


def triples_call(window, last, eb, vt, v, at, arep, ct, mask, ecol, lrow, total=None):
    _, count, block, _ = vt.shape
    groups, depth_rows, lanes = at.shape
    w = window
    tall, wide = pl.BlockSpec((1, lanes, block), lambda g: (g, 0, 0)), pl.BlockSpec((1, block, lanes), lambda g: (g, 0, 0))
    in_specs = [
        pl.BlockSpec(memory_space=pltpu.SMEM),
        pl.BlockSpec((1, count, block, LANE), lambda g: (w, 0, 0, 0)),
        pl.BlockSpec((1, block, count * block), lambda g: (w, 0, 0)),
        pl.BlockSpec((1, depth_rows, lanes), lambda g: (g, 0, 0)),
        pl.BlockSpec((1, 1, count, GROUP, lanes), lambda g: (w, g, 0, 0, 0)),
        pl.BlockSpec((1, 1) + ct.shape[2:], lambda g: (w, g, 0, 0, 0)),
        pl.BlockSpec(mask.shape, lambda g: (0, 0, 0)),
        pl.BlockSpec(ecol.shape, lambda g: (0, 0)),
        pl.BlockSpec((1, 1, 1, lanes), lambda g: (w, g, 0, 0)),
    ]
    operands = [eb[w : w + 1], vt, v, at, arep, ct, mask, ecol, lrow]
    if total is not None:
        in_specs.append(wide)
        operands.append(total)
    shape = (groups, lanes, block) if last else (groups, block, lanes)
    return pl.pallas_call(
        functools.partial(triples_kernel, last),
        grid=(groups,),
        in_specs=in_specs,
        out_specs=tall if last else wide,
        out_shape=jax.ShapeDtypeStruct(shape, jnp.float32),
        scratch_shapes=[pltpu.VMEM((count * block, lanes), jnp.bfloat16)],
        compiler_params=pltpu.CompilerParams(
            dimension_semantics=("arbitrary",), vmem_limit_bytes=40 * 1024 * 1024
        ),
        cost_estimate=pl.CostEstimate(
            flops=groups * count * block * lanes * 2 * (TILE + block) * 4,
            bytes_accessed=(arep.size + vt.size + v.size) * 2,
            transcendentals=groups * count * block * lanes,
        ),
        name="triples",
    )(*operands)


def swap_cores(x):
    return lax.ppermute(x, "irrep", [(0, 1), (1, 0)])


def across(x, bit):
    count = lax.axis_size("pair")
    return lax.ppermute(x, "pair", [(t, t ^ bit) for t in range(count)])


def pick(x, index):
    return lax.dynamic_index_in_dim(x, index, 0, keepdims=False)


def after(x, *others):
    return lax.optimization_barrier((x,) + others)[0]


class SlabPath:
    def __init__(self, owner, k_irrep, me, core):
        self.owner, self.k_irrep, self.core = owner, k_irrep, core
        self.windows = owner.shape[0]
        self.bits = [(me >> n) & 1 for n in range(4)]

    def from_here(self, bit):
        return ((self.owner >> bit) & 1) == self.bits[bit]

    def split_cores(self, slab):
        halves = slab.reshape((2, slab.shape[0] // 2) + slab.shape[1:])
        mine, theirs = pick(halves, self.core), swap_cores(pick(halves, 1 - self.core))
        same = self.bits[0] == self.core
        return jnp.where(same, mine, theirs), jnp.where(same, theirs, mine)

    def split_low(self, kept, came):
        def block(w, high, low):
            beta = (2 * high + low) ^ (self.k_irrep[w] & 3) ^ self.bits[0]
            return jnp.where(self.from_here(0)[w], pick(kept, beta), pick(came, beta))

        def blocks(low):
            return jnp.stack(
                [jnp.stack([block(w, high, low) for w in range(self.windows)]) for high in range(2)]
            )

        return blocks(self.bits[1]), blocks(1 - self.bits[1])

    def split_high(self, kept, came):
        here = self.from_here(1)[:, None, None]
        kept, leaving = [
            jnp.where(here, pick(kept, high), pick(came, high)) for high in (self.bits[2], 1 - self.bits[2])
        ]
        return kept, leaving

    def split_top(self, kept, came):
        blocks = jnp.where(self.from_here(2)[:, None, None], kept, came)
        mine, theirs = pick(blocks, self.core), swap_cores(pick(blocks, 1 - self.core))
        stays = (self.bits[3] ^ ((self.k_irrep[self.core] >> 2) & 1)) == self.core
        return jnp.where(stays, mine, theirs), jnp.where(stays, theirs, mine)

    def join(self, kept, came):
        block = jnp.where(self.from_here(3)[self.core], kept, came)
        other = swap_cores(block)
        first = self.core == 0
        return jnp.stack([jnp.where(first, block, other), jnp.where(first, other, block)])


def on_device_scatter(
    amplitudes, slabs, couplings, occ_energy, vir_energy, occ_irrep, pair_i, pair_j, window_k, owner
):
    betas, block = slabs.shape[1], slabs.shape[3]
    windows = window_k.shape[0]
    rows = block // lax.axis_size("irrep")
    share = rows * block
    chips = lax.axis_size("pair")
    local_pairs = pair_i.shape[0]
    pairs = chips * local_pairs
    groups = pairs // GROUP
    lanes, depth, starts = tile_plan(rows)
    me, core = lax.axis_index("pair"), lax.axis_index("irrep")
    gamma, m = me & 1, me >> 1
    k_irrep = occ_irrep[window_k]
    bf16 = jnp.bfloat16

    chunks = b_chunks(block)
    local = slabs[0, :, 0]
    path = SlabPath(owner, k_irrep, me, core)
    labels = jnp.pad(jnp.concatenate([pair_i, pair_j]), (0, LANE - 2 * local_pairs))
    labels = lax.all_to_all(jnp.broadcast_to(labels, (chips, 1, LANE)), "pair", 0, 0, tiled=True)
    kept_x, sent_x = zip(
        *[path.split_cores(local[:, :, first * block : (first + size) * block]) for first, size in chunks]
    )
    owner, window_k, occ_irrep, occ_energy, vir_energy, _ = lax.optimization_barrier(
        (owner, window_k, occ_irrep, occ_energy, vir_energy, sent_x[0])
    )
    k_irrep = occ_irrep[window_k]
    path.owner, path.k_irrep = owner, k_irrep
    x, leaving_x = [], []
    for leaving in sent_x:
        leaving_x.append(after(leaving, x[-1]) if x else leaving)
        x.append(across(leaving_x[-1], 1))
    kept_y, sent_y, kept_z, sent_z, kept_h, sent_h = {}, {}, {}, {}, {}, {}
    y, z, h, ready = {}, {}, {}, {}

    def to_low(chunk, *tokens):
        kept_y[chunk], sent_y[chunk] = path.split_low(kept_x[chunk], after(x[chunk], *tokens))
        y[chunk] = across(sent_y[chunk], 2)

    def to_high(chunk, *tokens):
        kept_z[chunk], sent_z[chunk] = path.split_high(kept_y[chunk], after(y[chunk], *tokens))
        z[chunk] = across(sent_z[chunk], 4)

    def to_top(chunk, *tokens):
        kept_h[chunk], sent_h[chunk] = path.split_top(kept_z[chunk], after(z[chunk], *tokens))
        h[chunk] = across(sent_h[chunk], 8)

    def arrive(chunk, *tokens):
        ready[chunk] = path.join(kept_h[chunk], after(h[chunk], *tokens))

    to_low(0, sent_x[0])
    to_low(1, sent_y[0])
    to_high(0, sent_y[1])

    pair_sym = occ_irrep[pair_i] ^ occ_irrep[pair_j]
    mine = lax.dynamic_slice_in_dim(after(amplitudes, sent_x[0]), core * share, share, 2)
    target = jnp.arange(chips, dtype=jnp.int32)
    wanted = jnp.stack([target >> 1] + [(target >> 1) ^ (target & 1) ^ k_irrep[w] for w in range(windows)], 1)
    index = wanted[:, :, None] ^ pair_sym[None, None, :]
    kinds = 1 + windows
    stored = mine.reshape(local_pairs * betas, share)
    index = index + betas * jnp.arange(local_pairs, dtype=jnp.int32)
    index = jnp.pad(index.reshape(chips, -1), ((0, 0), (0, 1)), constant_values=-1).reshape(-1)
    chosen = (index[:, None] == jnp.arange(stored.shape[0], dtype=jnp.int32)[None, :]).astype(bf16)
    sent = jnp.einsum("rh,hx->rx", chosen, stored)
    sent = sent.reshape(chips, kinds * local_pairs + 1, share)
    came = lax.all_to_all(sent, "pair", 0, 0, tiled=True)

    labels = after(labels, sent)
    both = labels[:, 0, : 2 * local_pairs]
    both = both.reshape(chips, 2, local_pairs).transpose(1, 0, 2).reshape(2, pairs)
    numbers = jnp.arange(pairs, dtype=jnp.int32)
    ahead = both[0][None, :] < both[0][:, None]
    tied = (both[0][None, :] == both[0][:, None]) & (numbers[None, :] < numbers[:, None])
    rank = jnp.sum((ahead | tied).astype(jnp.int32), axis=1)
    placed = (rank[None, :] == numbers[:, None]).astype(jnp.int32)
    order = jnp.sum(placed * numbers[None, :], axis=1)
    first = jnp.sum(placed * both[0][None, :], axis=1)
    second = jnp.sum(placed * both[1][None, :], axis=1)

    used = GROUP * rows
    coupled = jnp.where(gamma == core, couplings, swap_cores(couplings))
    chosen = (second.reshape(groups, GROUP)[:, :, None] == jnp.arange(occ_irrep.shape[0])).astype(bf16)
    coupled = jnp.einsum("gql,wljc->wgqjc", chosen, coupled)
    coupled = jnp.einsum("gpj,wgqjc->wgcpq", chosen, coupled)
    sym_j = occ_irrep[second].reshape(groups, GROUP)
    keep = (sym_j[None, :, :, None] ^ sym_j[None, :, None, :] ^ gamma ^ k_irrep[:, None, None, None]) == 0
    coupled = -(coupled * keep[:, :, None].astype(bf16))
    ct = jnp.stack(
        [coupled[:, :, :, s : s + depth].reshape(windows, groups, block, depth * GROUP) for s in starts], 2
    )

    alpha = occ_irrep[first] ^ occ_irrep[second] ^ m
    energy_a = lax.dynamic_slice_in_dim(vir_energy, core * rows, rows, 1)[alpha]
    base = occ_energy[first] + occ_energy[second]
    lrow = energy_a[None] - (base[None] + occ_energy[window_k][:, None])[:, :, None]
    lrow = lrow.reshape(windows, groups, 1, used)
    lrow = jnp.pad(lrow, ((0, 0), (0, 0), (0, 0), (0, lanes - used)), constant_values=1.0)
    source = (order // local_pairs) * (kinds * local_pairs + 1) + order % local_pairs
    source = source[None, :] + local_pairs * jnp.arange(kinds, dtype=jnp.int32)[:, None]
    came = after(came, sent_z[0], leaving_x[2], ct, lrow, source)
    came = came.reshape(chips * (kinds * local_pairs + 1), share)
    amps = came[source]
    amps = amps.reshape(kinds, groups, GROUP, rows, block)
    holes = lax.optimization_barrier(amps[1:].transpose(0, 1, 4, 2, 3))
    at = amps[0].transpose(0, 3, 1, 2).reshape(groups, block, used)
    at = jnp.pad(at, ((0, 0), (0, LANE - block), (0, lanes - used)))
    lane = jnp.arange(lanes, dtype=jnp.int32)
    spread = ((lane[None, :] % rows == jnp.arange(rows)[:, None]) & (lane < used)[None, :]).astype(bf16)
    lane_pair = lane // rows
    mask = jnp.stack([
        (jnp.repeat(start + jnp.arange(depth), GROUP)[:, None] == lane_pair[None, n * TILE : (n + 1) * TILE])
        for n, start in enumerate(starts)
    ]).astype(bf16)

    ecol = jnp.broadcast_to(pick(vir_energy, gamma)[:, None], (block, TILE))
    energy_b = vir_energy[m ^ gamma ^ k_irrep]

    eye = (jnp.arange(block)[:, None] == jnp.arange(LANE)[None, :]).astype(bf16)

    def spread_holes(chunk, *tokens):
        start, size = chunks[chunk]
        hole = after(holes, *tokens)[:, :, start : start + size]
        return jnp.einsum("wgbqa,ae->wgbqe", hole, spread)

    def run(chunk, w, v, total):
        start, size = chunks[chunk]
        vt = jnp.einsum("wdx,de->wxe", v, eye).reshape(windows, size, block, LANE)
        last = start + size == block and w == windows - 1
        energies = energy_b[:, start : start + size]
        return triples_call(w, last, energies, vt, v, at, areps[chunk], ct, mask, ecol, lrow, total)

    calls = [(chunk, w) for chunk in range(len(chunks)) for w in range(windows)]
    to_top(0, amps)
    to_high(1, sent_h[0])
    to_low(2, sent_z[1])
    at = after(at, sent_y[2], leaving_x[3])
    areps = {0: spread_holes(0, at)}
    ct = after(ct, areps[0])
    arrive(0, ct)
    to_top(1, ready[0])
    ready[0] = after(ready[0], sent_h[1])
    total = None
    for n, (chunk, w) in enumerate(calls):
        total = run(chunk, w, ready[chunk], total)
        if n == 0:
            arrive(1, total)
            areps[1] = spread_holes(1, total)
            total = after(total, ready[1])
        elif n == 1:
            to_high(2, total)
            to_low(3, sent_z[2])
            total = after(total, sent_y[3])
        elif n == 2:
            to_top(2, total)
            total = after(total, sent_h[2])
        elif n == 3:
            areps[2] = spread_holes(2, total)
            areps[3] = spread_holes(3, areps[2])
            to_high(3, areps[3])
            arrive(2, sent_z[3])
        elif n == 4:
            to_top(3, total)
            total = after(total, sent_h[3])
        elif n == 5:
            arrive(3, total)
    total = total[:, :used].reshape(pairs, share)[rank]
    cut = 8 if share % 8 == 0 else 1
    total = total.reshape(chips, local_pairs * cut, share // cut)
    came = lax.all_to_all(total, "pair", 0, 0, tiled=True)
    came = came.reshape(betas, 2, local_pairs, cut, share // cut)
    came = (came[:, 0] + came[:, 1]).reshape(betas, local_pairs, share)
    back = jnp.arange(betas, dtype=jnp.int32)[None, :] ^ pair_sym[:, None]
    return came[back, jnp.arange(local_pairs, dtype=jnp.int32)[:, None]]


def on_device(*args):
    betas, block = args[1].shape[1], args[1].shape[3]
    chips, cores = lax.axis_size("pair"), lax.axis_size("irrep")
    fits = lax.axis_size("vtile") == 1 and cores == 2 and betas == 8 and chips == betas * cores
    fits = fits and args[8].shape[0] == 2 and block % 2 == 0 and block < LANE
    fits = fits and all(size > 0 and size % 2 == 0 for _, size in b_chunks(block))
    if fits and 2 * args[6].shape[0] <= LANE:
        return on_device_scatter(*args)
    return on_device_gather(*args)


def solution(mesh):
    placed = (
        P("pair", None, None),
        P("pair", "vtile", "irrep", None, None),
        P(None, None, None, "irrep"),
        P(),
        P(),
        P(),
        P("pair"),
        P("pair"),
        P(),
        P(),
    )
    return jax.shard_map(
        on_device,
        mesh=mesh,
        in_specs=placed,
        out_specs=P("pair", "vtile", "irrep"),
        check_vma=False,
    )
```
